256 devices in a mesh: md: 64 (over z_hi, x, y), th: 4 (over z_lo, core).
Axes of the slice: x: 4, y: 4, z: 8 (z_hi: 4, z_lo: 2; z = z_hi * 2 + z_lo), core: 2. Of those that a mesh axis runs over, the one named last changes fastest.
Arguments:
- populations: float32 [19, 128, 128, 512], P(None, 'md', 'th'), may hold values from 0.01 to 0.52, as said below
- fibre_mask: int32 [128, 128, 512], P('md', 'th'), may hold values 0 or 1
- wire_open: int32 [128, 512], P('md'), may hold values 0 or 1
- fines: float32 [4, 128, 128, 512], P(None, 'md', None, 'th'), may hold values from 0.2 to 2
- diffusivity: float32 [4], replicated, may hold values from 20 to 400
- retention: float32 [4], replicated, may hold values from 0.05 to 0.5
Outputs:
- populations_out: float32 [19, 128, 128, 512], P(None, 'md', 'th')
- fines_out: float32 [4, 128, 128, 512], P(None, 'md', None, 'th')
The draws below stay inside these ranges and needn't reach their ends.
Inputs may be any that keep to these rules, and one draw needn't show every extreme that they name: `populations`: each population lies between 0.45 and 1.55 times its lattice weight.
All inputs are finite; a program needn't handle non-finite values. No bound on the sum of `fibre_mask` or of `wire_open` on one device may be relied on, other than what follows from the above.
Results may differ from the reference program's by a relative error of at most 0.0003.
Values sent between devices are 32-bit elements; how exact they have to be, the bound alone decides.
A program may use at most 64 MiB of HBM per device.

```python
import math
import jax
import jax.numpy as jnp
from jax import lax

NY = 512
FLOW_STEPS = 2
FINES_STEPS = 2
NX = 128
NZ = 128


VELOCITY_X = [0, 1, -1, 0, 0, 0, 0, 1, -1, 1, -1, 1, -1, 1, -1, 0, 0, 0, 0]


VELOCITY_Z = [0, 0, 0, 0, 0, 1, -1, 0, 0, 0, 0, 1, -1, -1, 1, 1, -1, -1, 1]


LATTICE_WEIGHTS = [1.0 / 3.0] + [1.0 / 18.0] * 6 + [1.0 / 36.0] * 12


def draw_populations(key, part):
    weight_table = jnp.array(LATTICE_WEIGHTS, jnp.float32)[:, None, None, None]
    mean_flow = 3.0 * (0.04 * jnp.array(VELOCITY_X, jnp.float32) - 0.03 * jnp.array(VELOCITY_Z, jnp.float32))
    jitter = jnp.clip(0.1 * jax.random.normal(key, (19, NX, NZ, NY), jnp.float32), -0.3, 0.3)
    return (weight_table * (1.0 + mean_flow[:, None, None, None] + jitter)).astype(jnp.float32)


def touch_ends(drawn, rng, smallest, top_value):
    place = [jax.random.randint(jax.random.fold_in(rng, axis), (), 0, length) for axis, length in enumerate(drawn.shape)]
    widest = drawn.shape.index(max(drawn.shape))
    neighbour = place[:widest] + [(place[widest] + 1) % drawn.shape[widest]] + place[widest + 1:]
    return drawn.at[tuple(place)].set(smallest).at[tuple(neighbour)].set(top_value)


def steps_of(key, shape, pieces, smallest, top_value):
    factor_of = 1.0
    for dim, parts in pieces:
        steps = jax.random.uniform(jax.random.fold_in(jax.random.fold_in(key, 6), dim), (parts,), jnp.float32, smallest / len(pieces), top_value / len(pieces))
        factor_of = factor_of * jnp.repeat(jnp.exp(steps), shape[dim] // parts).reshape((-1,) + (1,) * (len(shape) - 1 - dim))
    return factor_of


def setup_inputs(seed: int = 0) -> dict:
    splits = jax.random.split(jax.random.key(seed), 7)
    populations = draw_populations(jax.random.fold_in(splits[6], 71), 0)
    fibre_mask = touch_ends((jax.random.randint(splits[1], (NX, NZ, NY), 0, 4) < 1).astype(jnp.int32), jax.random.fold_in(splits[1], 1), 0, 1)
    wire_open = touch_ends((jax.random.randint(splits[2], (NX, NY), 0, 2) < 1).astype(jnp.int32), jax.random.fold_in(splits[2], 1), 0, 1)
    fines = jnp.clip(jnp.exp(math.log(2.0) - 2.3025851 * jax.random.uniform(splits[3], (4, NX, NZ, NY), jnp.float32) ** steps_of(splits[3], (4, NX, NZ, NY), ((1, 64), (3, 4)), -0.2, 0.2)), 0.2, 2.0)
    diffusivity = jnp.clip(jnp.exp(jax.random.uniform(splits[4], (4,), jnp.float32, math.log(20.0), math.log(400.0))), 20.0, 400.0)
    retention = jnp.clip(jnp.exp(jax.random.uniform(splits[5], (4,), jnp.float32, math.log(0.05), math.log(0.5))), 0.05, 0.5)
    return dict(populations=populations, fibre_mask=fibre_mask, wire_open=wire_open, fines=fines, diffusivity=diffusivity, retention=retention)


VELOCITIES = [(0, 0, 0), (1, 0, 0), (-1, 0, 0), (0, 1, 0), (0, -1, 0), (0, 0, 1), (0, 0, -1), (1, 1, 0), (-1, -1, 0), (1, -1, 0), (-1, 1, 0), (1, 0, 1), (-1, 0, -1), (1, 0, -1), (-1, 0, 1), (0, 1, 1), (0, -1, -1), (0, 1, -1), (0, -1, 1)]
WEIGHTS = [1.0 / 3.0] + [1.0 / 18.0] * 6 + [1.0 / 36.0] * 12
OPPOSITE = [0, 2, 1, 4, 3, 6, 5, 8, 7, 10, 9, 12, 11, 14, 13, 16, 15, 18, 17]
RELAXATION = 1.6
INLET_DENSITY = 1.03
OUTLET_DENSITY = 0.97
LATERAL_DIFFUSION = 0.1

def moments(state):
    mass = state[0]
    flux_x = jnp.zeros_like(state[0])
    flux_y = jnp.zeros_like(state[0])
    flux_z = jnp.zeros_like(state[0])
    for i in range(1, 19):
        step_x, step_y, step_z = VELOCITIES[i]
        mass = mass + state[i]
        flux_x = flux_x + step_x * state[i]
        flux_y = flux_y + step_y * state[i]
        flux_z = flux_z + step_z * state[i]
    return (mass, flux_x / mass, flux_y / mass, flux_z / mass)

def collide(state, solidity):
    mass, speed_x, speed_y, speed_z = moments(state)
    kinetic = 1.5 * (speed_x * speed_x + speed_y * speed_y + speed_z * speed_z)
    relaxed = []
    for i in range(19):
        step_x, step_y, step_z = VELOCITIES[i]
        projected = step_x * speed_x + step_y * speed_y + step_z * speed_z
        balance = WEIGHTS[i] * mass * (1.0 + 3.0 * projected + 4.5 * projected * projected - kinetic)
        updated = state[i] - RELAXATION * (state[i] - balance)
        relaxed.append(jnp.where(solidity > 0, state[OPPOSITE[i]], updated))
    return relaxed

def flow_fields(state, solidity):
    mass, speed_x, speed_y, speed_z = moments(state)
    fluid = 1.0 - solidity
    return jnp.stack([speed_x * fluid, speed_y * fluid, speed_z * fluid, solidity])

def explicit_part(concentration, local_flow, retention):
    centre = concentration[:, 1:-1, :, 1:-1]
    west_side = concentration[:, :-2, :, 1:-1]
    east_side = concentration[:, 2:, :, 1:-1]
    south_side = concentration[:, 1:-1, :, :-2]
    north_side = concentration[:, 1:-1, :, 2:]
    speed_x = local_flow[0][None]
    speed_y = local_flow[1][None]
    speed_z = local_flow[2][None]
    solidity = local_flow[3][None]
    below_cells = jnp.concatenate([centre[:, :, :1], centre[:, :, :-1]], axis=2)
    above_cells = jnp.concatenate([centre[:, :, 1:], centre[:, :, -1:]], axis=2)
    advect = jnp.where(speed_x > 0, speed_x * (centre - west_side), speed_x * (east_side - centre))
    advect = advect + jnp.where(speed_y > 0, speed_y * (centre - south_side), speed_y * (north_side - centre))
    advect = advect + jnp.where(speed_z > 0, speed_z * (centre - below_cells), speed_z * (above_cells - centre))
    lateral = LATERAL_DIFFUSION * (west_side + east_side + south_side + north_side - 4.0 * centre)
    return centre - advect + lateral - retention[:, None, None, None] * solidity * centre

def wrap_margin(values):
    return jnp.pad(values, ((0, 0), (1, 1), (0, 0), (1, 1)), mode='wrap')

def reference(populations, fibre_mask, wire_open, fines, diffusivity, retention):
    solidity = fibre_mask.astype(jnp.float32)
    open_cells = wire_open == 1
    state = populations
    for iteration in range(FLOW_STEPS):
        relaxed = collide(state, solidity)
        read = []
        for i in range(19):
            step_x, step_y, step_z = VELOCITIES[i]
            pulled = jnp.roll(relaxed[i], step_x, axis=0)
            pulled = jnp.roll(pulled, step_y, axis=2)
            if step_z == 1:
                boundary = jnp.where(open_cells, WEIGHTS[i] * OUTLET_DENSITY, relaxed[OPPOSITE[i]][:, 0, :])
                pulled = jnp.concatenate([boundary[:, None, :], pulled[:, :-1, :]], axis=1)
            elif step_z == -1:
                boundary = jnp.full_like(pulled[:, :1, :], WEIGHTS[i] * INLET_DENSITY)
                pulled = jnp.concatenate([pulled[:, 1:, :], boundary], axis=1)
            read.append(pulled)
        state = jnp.stack(read)
    flow_field = flow_fields(state, solidity)
    height = fines.shape[2]
    index = jnp.arange(height)
    column_ends = ((index == 0) | (index == height - 1)).astype(diffusivity.dtype)
    main_band = 1.0 + diffusivity[:, None] * (2.0 - column_ends[None, :])
    lower_band = jnp.where(index[None, :] == 0, 0.0, -diffusivity[:, None])
    upper_band = jnp.where(index[None, :] == height - 1, 0.0, -diffusivity[:, None])
    concentration = fines
    for iteration in range(FINES_STEPS):
        values = explicit_part(wrap_margin(concentration), flow_field, retention)
        right_side = jnp.transpose(values, (0, 2, 1, 3)).reshape(values.shape[0], height, -1)
        solved = lax.linalg.tridiagonal_solve(lower_band, main_band, upper_band, right_side)
        solved = solved.reshape(values.shape[0], height, values.shape[1], values.shape[3])
        concentration = jnp.transpose(solved, (0, 2, 1, 3))
    return (state, concentration)
```

```python
import functools

import jax
import jax.numpy as jnp
from jax import lax
from jax.experimental import pallas as pl
from jax.experimental.pallas import tpu as pltpu
from jax.sharding import PartitionSpec as P

VELOCITIES = [
    (0, 0, 0), (1, 0, 0), (-1, 0, 0), (0, 1, 0), (0, -1, 0), (0, 0, 1), (0, 0, -1),
    (1, 1, 0), (-1, -1, 0), (1, -1, 0), (-1, 1, 0), (1, 0, 1), (-1, 0, -1), (1, 0, -1),
    (-1, 0, 1), (0, 1, 1), (0, -1, -1), (0, 1, -1), (0, -1, 1),
]
WEIGHTS = [1.0 / 3.0] + [1.0 / 18.0] * 6 + [1.0 / 36.0] * 12
OPPOSITE = [0, 2, 1, 4, 3, 6, 5, 8, 7, 10, 9, 12, 11, 14, 13, 16, 15, 18, 17]
RELAXATION = 1.6
INLET_DENSITY = 1.03
OUTLET_DENSITY = 0.97
LATERAL_DIFFUSION = 0.1

PLUS = [1, 7, 9, 11, 13]
MINUS = [2, 8, 10, 12, 14]
ZERO = [0, 3, 4, 5, 6, 15, 16, 17, 18]
SLOT = {i: k for k, i in enumerate(PLUS + MINUS + ZERO)}
UP = [5, 15, 18, 11, 14]
DOWN = [6, 16, 17, 12, 13]

MESH = pl.DeviceIdType.MESH
LANES = 128
NT = 4
TOP = 8


def moments(f):
    def add(items):
        items = list(items)
        while len(items) > 1:
            items = [a + b for a, b in zip(items[::2], items[1::2])] + (
                [items[-1]] if len(items) % 2 else []
            )
        return items[0]

    mass = add(f)
    flux = []
    for axis in range(3):
        plus = add([f[i] for i in range(19) if VELOCITIES[i][axis] == 1])
        minus = add([f[i] for i in range(19) if VELOCITIES[i][axis] == -1])
        flux.append(plus - minus)
    inverse = 1.0 / mass
    return mass, flux[0] * inverse, flux[1] * inverse, flux[2] * inverse


def collide(f, solid):
    mass, ux, uy, uz = moments(f)
    base = 1.0 - 1.5 * (ux * ux + uy * uy + uz * uz)
    out = [None] * 19
    out[0] = jnp.where(solid, f[0], (1.0 - RELAXATION) * f[0] + (RELAXATION * WEIGHTS[0]) * (mass * base))
    scaled = {w: (RELAXATION * w) * mass for w in (WEIGHTS[1], WEIGHTS[7])}
    for i in range(1, 19, 2):
        j = OPPOSITE[i]
        cx, cy, cz = VELOCITIES[i]
        terms = [u if c > 0 else -u for c, u in ((cx, ux), (cy, uy), (cz, uz)) if c != 0]
        p = functools.reduce(lambda a, b: a + b, terms)
        m = scaled[WEIGHTS[i]]
        even = m * (base + 4.5 * (p * p))
        odd = m * (3.0 * p)
        out[i] = jnp.where(solid, f[j], (1.0 - RELAXATION) * f[i] + (even + odd))
        out[j] = jnp.where(solid, f[i], (1.0 - RELAXATION) * f[j] + (even - odd))
    return out


def kernel(
    pops, mask, wire, fines, diff, ret, pops_out, fines_out,
    F, R, M, S, Sall, V, Vall, B, ZU, ZD, RU, RD, W, Q, C, X, G, YP, YW, YE,
    in_sem, out_sem, xs_s, xs_r, zs_s, zs_r, ss_s, ss_r, vs_s, vs_r, q_s, q_r, y_s, y_r,
):
    md = lax.axis_index("md")
    th = lax.axis_index("th")
    nmd = lax.axis_size("md")
    right, left = lax.rem(md + 1, nmd), lax.rem(md + nmd - 1, nmd)
    up, dn = lax.rem(th + 1, 4), lax.rem(th + 3, 4)
    peers = [lax.rem(th + d, 4) for d in (1, 2, 3)]

    loads = [
        pltpu.make_async_copy(fines, Q.at[0, :, 1:3, 8:136, :], in_sem.at[0]),
    ]
    for t in range(NT):
        loads.append(pltpu.make_async_copy(
            mask.at[:, :, t * LANES:(t + 1) * LANES], M.at[:, t], in_sem.at[1 + t]))
    for t in range(NT):
        loads.append(pltpu.make_async_copy(
            pops.at[:, :, :, t * LANES:(t + 1) * LANES], F.at[:, :, t], in_sem.at[5 + t]))
    for c in loads:
        c.start()

    barrier = pltpu.get_barrier_semaphore()
    friends = [(right, th), (left, th)] + [(md, p) for p in peers]
    friends += [(m, t) for m in (right, left) for t in (up, dn)]
    for d in friends:
        pl.semaphore_signal(barrier, inc=1, device_id=d, device_id_type=MESH)

    lane = lax.broadcasted_iota(jnp.int32, (8, LANES), 1)
    sub = lax.broadcasted_iota(jnp.int32, (8, LANES), 0)

    def remote(src, dst, s, r, dev):
        return pltpu.make_async_remote_copy(
            src_ref=src, dst_ref=dst, send_sem=s, recv_sem=r, device_id=dev, device_id_type=MESH)

    for x in range(2):
        for t in range(NT):
            W[x * NT + t:x * NT + t + 1, :] = wire[x:x + 1, t * LANES:(t + 1) * LANES]

    def pack_columns(buf, s, step):
        def body(k, carry):
            east, west = carry
            x, zc = k // 16, lax.rem(k, 16)
            c = Q[buf, s, x + 1, pl.ds(pl.multiple_of(8 + zc * 8, 8), 8), :]
            here = lane == k
            east = jnp.where(here, pltpu.roll(c, lax.rem(k + 1, LANES), 1), east)
            west = jnp.where(here, pltpu.roll(c, k, 1), west)
            return east, west
        zero = jnp.zeros((8, LANES), jnp.float32)
        east, west = lax.fori_loop(0, 32, body, (zero, zero))
        YP[step, s, 0] = east
        YP[step, s, 1] = west

    def fine_sends(step, s):
        return [
            remote(Q.at[step, s, 2, 8:136, :], Q.at[step, s, 0, 8:136, :], q_s.at[step, s, 0], q_r.at[step, s, 0], (right, th)),
            remote(Q.at[step, s, 1, 8:136, :], Q.at[step, s, 3, 8:136, :], q_s.at[step, s, 1], q_r.at[step, s, 1], (left, th)),
            remote(YP.at[step, s, 0], YW.at[step, s], y_s.at[step, s, 0], y_r.at[step, s, 0], (md, up)),
            remote(YP.at[step, s, 1], YE.at[step, s], y_s.at[step, s, 1], y_r.at[step, s, 1], (md, dn)),
        ]

    loads[0].wait()
    for s in range(4):
        pack_columns(0, s, 0)
    for t in range(NT):
        loads[1 + t].wait()
    S[...] = M[...].astype(jnp.float32)

    pl.semaphore_wait(barrier, len(friends))
    fine0 = [fine_sends(0, s) for s in range(4)]
    for s in range(4):
        for c in fine0[s]:
            c.start()
    my_rows = pl.ds(pl.multiple_of(th * 32, 32), 32)
    solids = [
        remote(S.at[:, p], Sall.at[:, my_rows, :], ss_s.at[k], ss_r.at[k], (md, p))
        for k, p in enumerate(peers)
    ]
    for c in solids:
        c.start()
    for x in range(2):
        Sall[x, my_rows, :] = S[x, th]

    def put(e, x, t, z, out):
        rows = pl.ds(pl.multiple_of(8 + z * 8, 8), 8)
        for i in range(19):
            cy = VELOCITIES[i][1]
            k = SLOT[i]
            if cy == 0:
                R[e, k, x + 1, t, rows, :] = out[i]
            elif cy == 1:
                v = pltpu.roll(out[i], 1, 1)
                R[e, k, x + 1, t, rows, 1:LANES] = v[:, 1:LANES]
                R[e, k, x + 1, lax.rem(t + 1, NT), rows, 0:1] = v[:, 0:1]
            else:
                v = pltpu.roll(out[i], LANES - 1, 1)
                R[e, k, x + 1, t, rows, 0:LANES - 1] = v[:, 0:LANES - 1]
                R[e, k, x + 1, lax.rem(t + 3, NT), rows, LANES - 1:LANES] = v[:, LANES - 1:LANES]
        for k in range(5):
            B[k, x * NT + t] = out[DOWN[k]]

    def solid_at(x, t, z):
        return S[x, t, pl.ds(pl.multiple_of(z * 8, 8), 8), :] > 0

    def chunks(body):
        def step(n, _):
            z = 3 - n // 8
            r = lax.rem(n, 8)
            body(r // NT, lax.rem(r, NT), z)
            return 0
        lax.fori_loop(0, 32, step, 0)

    def pull(e, x, t, z):
        f = []
        for i in range(19):
            cx, _, cz = VELOCITIES[i]
            f.append(R[e, SLOT[i], x + 1 - cx, t, pl.ds(8 + z * 8 - cz, 8), :])
        return f

    def exchange(e):
        for k in range(5):
            for x in range(2):
                for t in range(NT):
                    r = x * NT + t
                    ZU[e, k, r:r + 1, :] = R[e, SLOT[UP[k]], x + 1, t, 39:40, :]
                    ZD[e, k, r:r + 1, :] = R[e, SLOT[DOWN[k]], x + 1, t, 8:9, :]
        out = [
            remote(R.at[e, 0:5, 2, :, 8:40, :], R.at[e, 0:5, 0, :, 8:40, :], xs_s.at[e, 0], xs_r.at[e, 0], (right, th)),
            remote(R.at[e, 5:10, 1, :, 8:40, :], R.at[e, 5:10, 3, :, 8:40, :], xs_s.at[e, 1], xs_r.at[e, 1], (left, th)),
            remote(ZU.at[e], RU.at[e, 0:5], zs_s.at[e, 0], zs_r.at[e, 0], (md, up)),
            remote(ZU.at[e, 3], RU.at[e, 5], zs_s.at[e, 1], zs_r.at[e, 1], (right, up)),
            remote(ZU.at[e, 4], RU.at[e, 6], zs_s.at[e, 2], zs_r.at[e, 2], (left, up)),
            remote(ZD.at[e], RD.at[e, 0:5], zs_s.at[e, 3], zs_r.at[e, 3], (md, dn)),
            remote(ZD.at[e, 4], RD.at[e, 5], zs_s.at[e, 4], zs_r.at[e, 4], (right, dn)),
            remote(ZD.at[e, 3], RD.at[e, 6], zs_s.at[e, 5], zs_r.at[e, 5], (left, dn)),
        ]
        for c in out:
            c.start()
        return out

    def edges(e, sends):
        for c in sends[2:]:
            c.wait_recv()
        low = sub < NT
        is_open = W[...] == 1
        for k in range(5):
            for vertical, pop in ((0, UP[k]), (1, DOWN[k])):
                src = RD if vertical else RU
                cx = VELOCITIES[pop][0]
                tile = src[e, k]
                if cx == 1:
                    tile = pltpu.roll(jnp.where(low, tile, src[e, 5]), NT, 0)
                elif cx == -1:
                    tile = pltpu.roll(jnp.where(low, src[e, 6], tile), NT, 0)
                if vertical:
                    tile = jnp.where(th == 3, WEIGHTS[pop] * INLET_DENSITY, tile)
                    row = 40
                else:
                    solid_wire = jnp.concatenate([B[k, r, 0:1, :] for r in range(8)], axis=0)
                    wall = jnp.where(is_open, WEIGHTS[pop] * OUTLET_DENSITY, solid_wire)
                    tile = jnp.where(th == 0, wall, tile)
                    row = 7
                for x in range(2):
                    for t in range(NT):
                        r = x * NT + t
                        R[e, SLOT[pop], x + 1 - cx, t, row:row + 1, :] = tile[r:r + 1, :]
        for c in sends[:2]:
            c.wait_recv()

    for t in range(NT):
        loads[5 + t].wait()

    def first(x, t, z):
        rows = pl.ds(pl.multiple_of(z * 8, 8), 8)
        put(0, x, t, z, collide([F[i, x, t, rows, :] for i in range(19)], solid_at(x, t, z)))

    chunks(first)
    sent0 = exchange(0)

    def inverse(n, _):
        s, zc = n // 16, lax.rem(n, 16)
        d = jnp.full((8, LANES), diff[s], jnp.float32)
        h = 0.5 * lax.rsqrt(d)
        theta = 2.0 * jnp.log1p(h + h * h / (1.0 + jnp.sqrt(1.0 + h * h)))
        i = (sub + zc * 8).astype(jnp.float32)
        j = lane.astype(jnp.float32)
        gap = jnp.abs(i - j)
        total = i + j + 1.0
        full = 2.0 * LANES
        top = jnp.exp(-theta * gap) + jnp.exp(-theta * (full - gap))
        top = top + (jnp.exp(-theta * total) + jnp.exp(-theta * (full - total)))
        g = top / (jnp.sqrt(4.0 * d + 1.0) * (1.0 - jnp.exp(-theta * full)))
        G[s, pl.ds(pl.multiple_of(zc * 8, 8), 8), :] = g
        return 0

    lax.fori_loop(0, 64, inverse, 0)

    edges(0, sent0)

    def second(x, t, z):
        put(1, x, t, z, collide(pull(0, x, t, z), solid_at(x, t, z)))

    chunks(second)
    sent1 = exchange(1)
    edges(1, sent1)

    def third(x, t, z):
        f = pull(1, x, t, z)
        rows = pl.ds(pl.multiple_of(z * 8, 8), 8)
        for i in range(19):
            F[i, x, t, rows, :] = f[i]
        _, ux, uy, uz = moments(f)
        fluid = 1.0 - S[x, t, rows, :]
        V[0, x, t, rows, :] = ux * fluid
        V[1, x, t, rows, :] = uy * fluid
        V[2, x, t, rows, :] = uz * fluid

    chunks(third)
    speeds = [
        remote(V.at[:, :, p], Vall.at[:, :, my_rows, :], vs_s.at[k], vs_r.at[k], (md, p))
        for k, p in enumerate(peers)
    ]
    for c in speeds:
        c.start()
    stores = []
    for t in range(NT):
        stores.append(pltpu.make_async_copy(
            F.at[:, :, t], pops_out.at[:, :, :, t * LANES:(t + 1) * LANES], out_sem.at[t]))
    for c in stores:
        c.start()
    for a in range(3):
        for x in range(2):
            Vall[a, x, my_rows, :] = V[a, x, th]

    for c in solids:
        c.wait_recv()
    for c in speeds:
        c.wait_recv()

    def coefficients(n, _):
        x, zc = n // 16, lax.rem(n, 16)
        rows = pl.ds(pl.multiple_of(zc * 8, 8), 8)
        ux, uy, uz = [Vall[a, x, rows, :] for a in range(3)]
        C[0, x, rows, :] = (1.0 - 4.0 * LATERAL_DIFFUSION) - (jnp.abs(ux) + jnp.abs(uy) + jnp.abs(uz))
        C[1, x, rows, :] = LATERAL_DIFFUSION + jnp.maximum(ux, 0.0)
        C[2, x, rows, :] = LATERAL_DIFFUSION - jnp.minimum(ux, 0.0)
        C[3, x, rows, :] = LATERAL_DIFFUSION + jnp.maximum(uy, 0.0)
        C[4, x, rows, :] = LATERAL_DIFFUSION - jnp.minimum(uy, 0.0)
        C[5, x, rows, :] = jnp.maximum(uz, 0.0)
        C[6, x, rows, :] = -jnp.minimum(uz, 0.0)
        return 0

    lax.fori_loop(0, 32, coefficients, 0)

    def transport(step, s, sends):
        for x in range(2):
            Q[step, s, x + 1, 7:8, :] = Q[step, s, x + 1, 8:9, :]
            Q[step, s, x + 1, 136:137, :] = Q[step, s, x + 1, 135:136, :]
        for c in sends:
            c.wait_recv()
        west_in = YW[step, s]
        east_in = YE[step, s]

        def explicit(n, _):
            x, zc = n // 16, lax.rem(n, 16)
            rows = pl.ds(pl.multiple_of(zc * 8, 8), 8)
            held = pl.ds(pl.multiple_of(8 + zc * 8, 8), 8)
            c = Q[step, s, x + 1, held, :]
            below = Q[step, s, x + 1, pl.ds(7 + zc * 8, 8), :]
            above = Q[step, s, x + 1, pl.ds(9 + zc * 8, 8), :]
            south = jnp.where(lane == 0, pltpu.roll(west_in, lax.rem(LANES - n, LANES), 1), pltpu.roll(c, 1, 1))
            north = jnp.where(lane == LANES - 1, pltpu.roll(east_in, LANES - 1 - n, 1), pltpu.roll(c, LANES - 1, 1))
            value = c * (C[0, x, rows, :] - ret[s] * Sall[x, rows, :])
            value += Q[step, s, x, held, :] * C[1, x, rows, :]
            value += Q[step, s, x + 2, held, :] * C[2, x, rows, :]
            value += south * C[3, x, rows, :]
            value += north * C[4, x, rows, :]
            value += below * C[5, x, rows, :]
            value += above * C[6, x, rows, :]
            X[x, rows, :] = value
            return 0

        lax.fori_loop(0, 32, explicit, 0)
        g = G[s]
        g_hi = g.astype(jnp.bfloat16)
        g_lo = (g - g_hi.astype(jnp.float32)).astype(jnp.bfloat16)
        for x in range(2):
            v = X[x]
            v_hi = v.astype(jnp.bfloat16)
            v_lo = (v - v_hi.astype(jnp.float32)).astype(jnp.bfloat16)
            q = jnp.dot(g_lo, v_hi, preferred_element_type=jnp.float32)
            q += jnp.dot(g_hi, v_lo, preferred_element_type=jnp.float32)
            q += jnp.dot(g_hi, v_hi, preferred_element_type=jnp.float32)
            if step == 0:
                Q[1, s, x + 1, 8:136, :] = q
            else:
                X[2 + 2 * s + x] = q

    fine1 = []
    for s in range(4):
        transport(0, s, fine0[s])
        pack_columns(1, s, 1)
        sends = fine_sends(1, s)
        for c in sends:
            c.start()
        fine1.append(sends)
    for s in range(4):
        transport(1, s, fine1[s])
        c = pltpu.make_async_copy(X.at[2 + 2 * s:4 + 2 * s], fines_out.at[s], out_sem.at[NT + s])
        c.start()
        stores.append(c)

    for c in sent0 + sent1 + solids + speeds:
        c.wait_send()
    for group in fine0 + fine1:
        for c in group:
            c.wait_send()
    for c in stores:
        c.wait()


def on_device(populations, fibre_mask, wire_open, fines, diffusivity, retention):
    any_ = pl.BlockSpec(memory_space=pl.ANY)
    smem = pl.BlockSpec(memory_space=pltpu.SMEM)
    f32 = jnp.float32
    dma = pltpu.SemaphoreType.DMA
    return pl.pallas_call(
        kernel,
        out_shape=(
            jax.ShapeDtypeStruct(populations.shape, f32),
            jax.ShapeDtypeStruct(fines.shape, f32),
        ),
        in_specs=[any_, any_, pl.BlockSpec(memory_space=pltpu.VMEM), any_, smem, smem],
        out_specs=(any_, any_),
        scratch_shapes=[
            pltpu.VMEM((19, 2, NT, 32, LANES), f32),
            pltpu.VMEM((2, 19, 4, NT, 48, LANES), f32),
            pltpu.VMEM((2, NT, 32, LANES), jnp.int32),
            pltpu.VMEM((2, NT, 32, LANES), f32),
            pltpu.VMEM((2, 128, LANES), f32),
            pltpu.VMEM((3, 2, NT, 32, LANES), f32),
            pltpu.VMEM((3, 2, 128, LANES), f32),
            pltpu.VMEM((5, 8, 8, LANES), f32),
            pltpu.VMEM((2, 5, 8, LANES), f32),
            pltpu.VMEM((2, 5, 8, LANES), f32),
            pltpu.VMEM((2, 7, 8, LANES), f32),
            pltpu.VMEM((2, 7, 8, LANES), f32),
            pltpu.VMEM((8, LANES), jnp.int32),
            pltpu.VMEM((2, 4, 4, 144, LANES), f32),
            pltpu.VMEM((7, 2, 128, LANES), f32),
            pltpu.VMEM((10, 128, LANES), f32),
            pltpu.VMEM((4, 128, LANES), f32),
            pltpu.VMEM((2, 4, 2, 8, LANES), f32),
            pltpu.VMEM((2, 4, 8, LANES), f32),
            pltpu.VMEM((2, 4, 8, LANES), f32),
            dma((9,)), dma((8,)),
            dma((2, 2)), dma((2, 2)),
            dma((2, 6)), dma((2, 6)),
            dma((3,)), dma((3,)),
            dma((3,)), dma((3,)),
            dma((2, 4, 2)), dma((2, 4, 2)),
            dma((2, 4, 2)), dma((2, 4, 2)),
        ],
        compiler_params=pltpu.CompilerParams(
            collective_id=0, has_side_effects=True, vmem_limit_bytes=56 * 1024 * 1024),
        name="drainage",
    )(populations, fibre_mask, wire_open, fines, diffusivity, retention)


def solution(mesh):
    return jax.shard_map(
        on_device,
        mesh=mesh,
        in_specs=(
            P(None, "md", "th", None), P("md", "th", None), P("md", None),
            P(None, "md", None, "th"), P(), P(),
        ),
        out_specs=(P(None, "md", "th", None), P(None, "md", None, "th")),
        check_vma=False,
    )
```

```python
import functools

import jax
import jax.numpy as jnp
from jax import lax
from jax.experimental import pallas as pl
from jax.experimental.pallas import tpu as pltpu
from jax.sharding import PartitionSpec as P

VELOCITIES = [
    (0, 0, 0), (1, 0, 0), (-1, 0, 0), (0, 1, 0), (0, -1, 0), (0, 0, 1), (0, 0, -1),
    (1, 1, 0), (-1, -1, 0), (1, -1, 0), (-1, 1, 0), (1, 0, 1), (-1, 0, -1), (1, 0, -1),
    (-1, 0, 1), (0, 1, 1), (0, -1, -1), (0, 1, -1), (0, -1, 1),
]
WEIGHTS = [1.0 / 3.0] + [1.0 / 18.0] * 6 + [1.0 / 36.0] * 12
OPPOSITE = [0, 2, 1, 4, 3, 6, 5, 8, 7, 10, 9, 12, 11, 14, 13, 16, 15, 18, 17]
RELAXATION = 1.6
INLET_DENSITY = 1.03
OUTLET_DENSITY = 0.97
LATERAL_DIFFUSION = 0.1

PLUS = [1, 7, 9, 11, 13]
MINUS = [2, 8, 10, 12, 14]
ZERO = [0, 3, 4, 5, 6, 15, 16, 17, 18]
SLOT = {i: k for k, i in enumerate(PLUS + MINUS + ZERO)}
UP = [5, 15, 18, 11, 14]
DOWN = [6, 16, 17, 12, 13]

MESH = pl.DeviceIdType.MESH
LANES = 128
NT = 4
TOP = 8


def total(items):
    items = list(items)
    while len(items) > 1:
        items = [a + b for a, b in zip(items[::2], items[1::2])] + (
            [items[-1]] if len(items) % 2 else []
        )
    return items[0]


PAIRS = list(range(1, 19, 2))


def signed(terms):
    plus = [v for c, v in terms if c > 0]
    minus = [v for c, v in terms if c < 0]
    return total(plus) - total(minus) if minus else total(plus)


def pair_moments(f):
    even = {i: f[i] + f[i + 1] for i in PAIRS}
    odd = {i: f[i] - f[i + 1] for i in PAIRS}
    mass = total([f[0]] + [even[i] for i in PAIRS])
    flux = [
        signed([(VELOCITIES[i][a], odd[i]) for i in PAIRS if VELOCITIES[i][a]]) for a in range(3)
    ]
    return even, odd, mass, flux


def collide(f, solid):
    even, odd, mass, flux = pair_moments(f)
    scale = (4.5 ** 0.5) / mass
    px, py, pz = [v * scale for v in flux]
    base = 1.0 - (1.0 / 3.0) * (px * px + py * py + pz * pz)
    keep = 1.0 - RELAXATION
    k_even = jnp.where(solid, 0.5, 0.5 * keep)
    k_odd = jnp.where(solid, -0.5, 0.5 * keep)
    m_diag = jnp.where(solid, 0.0, (RELAXATION * WEIGHTS[7]) * mass)
    m_axis = m_diag + m_diag
    odd_diag, odd_axis = (2.0 ** 0.5) * m_diag, (2.0 ** 0.5) * m_axis
    out = [None] * 19
    out[0] = jnp.where(solid, 1.0, keep) * f[0] + (WEIGHTS[0] / WEIGHTS[7]) * (m_diag * base)
    for i in PAIRS:
        p = signed([(c, v) for c, v in zip(VELOCITIES[i], (px, py, pz)) if c])
        axis = i < 7
        a = k_even * even[i] + (m_axis if axis else m_diag) * (base + p * p)
        b = k_odd * odd[i] + (odd_axis if axis else odd_diag) * p
        out[i] = a + b
        out[i + 1] = a - b
    return out


DIRECT = 3


def kernel(
    pops, mask, wire_hbm, fines, diff_hbm, ret_hbm, pops_out, fines_out,
    wire, diff, ret, F, R0, R1, M, S, Sall, V, Vall, B, ZU, ZD, RU, RD, W, Q0, Q1, C, X, G, GB, YP, YW, YE, RB, QB,
    in_sem, xs_s, xs_r, zs_s, zs_r, ss_s, ss_r, vs_s, vs_r, q_s, q_r, y_s, y_r,
    rb_r, fw_s, qb_r, qf_s,
):
    md = lax.axis_index("md")
    th = lax.axis_index("th")
    nmd = lax.axis_size("md")
    right, left = lax.rem(md + 1, nmd), lax.rem(md + nmd - 1, nmd)
    up, dn = lax.rem(th + 1, 4), lax.rem(th + 3, 4)
    peers = [lax.rem(th + d, 4) for d in (1, 2, 3)]
    R = (R0, R1)
    Q = (Q0, Q1)
    first = lax.rem(md, 16) == 0
    last = lax.rem(md, 16) == 15
    corner = first | last
    opposite = jnp.where(first, lax.rem(md + 15, nmd), lax.rem(md + nmd - 15, nmd))
    ahead, behind = lax.rem(md + 16, nmd), lax.rem(md + nmd - 16, nmd)

    loads = [
        pltpu.make_async_copy(fines, Q0.at[:, 1:3, 8:136, :], in_sem.at[0]),
    ]
    for t in range(NT):
        loads.append(pltpu.make_async_copy(
            mask.at[:, :, t * LANES:(t + 1) * LANES], M.at[:, t], in_sem.at[1 + t]))
    for t in range(NT):
        loads.append(pltpu.make_async_copy(
            pops.at[:, :, :, t * LANES:(t + 1) * LANES], F.at[:, :, t], in_sem.at[5 + t]))
    small = [
        pltpu.make_async_copy(a, b, in_sem.at[9 + k])
        for k, (a, b) in enumerate(((wire_hbm, wire), (diff_hbm, diff), (ret_hbm, ret)))
    ]
    for c in loads + small:
        c.start()

    barrier = pltpu.get_barrier_semaphore()
    friends = [(right, th), (left, th)] + [(md, p) for p in peers]
    friends += [(m, t) for m in (right, left) for t in (up, dn)]
    for d in friends:
        pl.semaphore_signal(barrier, inc=1, device_id=d, device_id_type=MESH)

    @pl.when(corner)
    def _():
        for m in (opposite, ahead, behind):
            pl.semaphore_signal(barrier, inc=1, device_id=(m, th), device_id_type=MESH)

    lane = lax.broadcasted_iota(jnp.int32, (8, LANES), 1)
    sub = lax.broadcasted_iota(jnp.int32, (8, LANES), 0)

    def remote(src, dst, s, r, dev):
        return pltpu.make_async_remote_copy(
            src_ref=src, dst_ref=dst, send_sem=s, recv_sem=r, device_id=dev, device_id_type=MESH)

    def rows8(z):
        return pl.ds(pl.multiple_of(z * 8, 8), 8)

    for c in small:
        c.wait()
    for x in range(2):
        for t in range(NT):
            W[x * NT + t:x * NT + t + 1, :] = wire[x:x + 1, t * LANES:(t + 1) * LANES]

    def pack_columns(step, s):
        east = west = jnp.zeros((8, LANES), jnp.float32)
        for x in range(2):
            for zc in range(16):
                k = x * 16 + zc
                c = Q[step][s, x + 1, 8 + zc * 8:16 + zc * 8, :]
                east = jnp.where(lane == k, pltpu.roll(c, k + 1, 1), east)
                west = jnp.where(lane == k, pltpu.roll(c, k, 1) if k else c, west)
        YP[step, s, 0] = east
        YP[step, s, 1] = west

    def fine_copies(step, s):
        q = Q[step]
        return [
            remote(q.at[s, 2, 8:136, :], q.at[s, 0, 8:136, :], q_s.at[step, s, 0], q_r.at[step, s, 0], (right, th)),
            remote(q.at[s, 1, 8:136, :], q.at[s, 3, 8:136, :], q_s.at[step, s, 1], q_r.at[step, s, 1], (left, th)),
            remote(YP.at[step, s, 0], YW.at[step, s], y_s.at[step, s, 0], y_r.at[step, s, 0], (md, up)),
            remote(YP.at[step, s, 1], YE.at[step, s], y_s.at[step, s, 1], y_r.at[step, s, 1], (md, dn)),
        ]

    def start_fines(step, s):
        q = Q[step]
        k = s // 2
        relayed = lax.rem(s, 2) == 0
        copies = fine_copies(step, s)
        for side, edge, plane in ((0, last, 2), (1, first, 1)):
            via = relayed & edge

            @pl.when(via)
            def _():
                remote(q.at[s, plane, 8:136, :], QB.at[step, k], q_s.at[step, s, side], qb_r.at[step, k], (opposite, th)).start()

            @pl.when(jnp.logical_not(via))
            def _():
                copies[side].start()

        copies[2].start()
        copies[3].start()

    def fine_forwards(step, side, dev, plane):
        return [
            remote(QB.at[step, k], Q[step].at[2 * k, plane, 8:136, :], qf_s.at[step, k], q_r.at[step, 2 * k, side], (dev, th))
            for k in range(2)
        ]

    def forward_fines(step):
        arrivals = [
            remote(Q[step].at[2 * k, 1, 8:136, :], QB.at[step, k], q_s.at[step, 2 * k, 0], qb_r.at[step, k], (opposite, th))
            for k in range(2)
        ]

        @pl.when(first)
        def _():
            for a, c in zip(arrivals, fine_forwards(step, 0, ahead, 0)):
                a.wait_recv()
                c.start()

        @pl.when(last)
        def _():
            for a, c in zip(arrivals, fine_forwards(step, 1, behind, 3)):
                a.wait_recv()
                c.start()

    loads[0].wait()

    def pack_first(s, _):
        pack_columns(0, s)
        return 0

    lax.fori_loop(0, 4, pack_first, 0)
    for t in range(NT):
        loads[1 + t].wait()
    S[...] = M[...].astype(jnp.float32)

    @pl.when(corner)
    def _():
        pl.semaphore_wait(barrier, len(friends) + 3)

    @pl.when(jnp.logical_not(corner))
    def _():
        pl.semaphore_wait(barrier, len(friends))

    def send_first(s, _):
        start_fines(0, s)
        return 0

    lax.fori_loop(0, 4, send_first, 0)
    my_rows = pl.ds(pl.multiple_of(th * 32, 32), 32)
    solids = [
        remote(S.at[:, p], Sall.at[:, my_rows, :], ss_s.at[k], ss_r.at[k], (md, p))
        for k, p in enumerate(peers)
    ]
    for c in solids:
        c.start()
    for x in range(2):
        Sall[x, my_rows, :] = S[x, th]

    def put(e, x, t, z, out):
        rows = pl.ds(pl.multiple_of(8 + z * 8, 8), 8)
        r = R[e]
        for i in range(19):
            cy = VELOCITIES[i][1]
            k = SLOT[i]
            if cy == 0:
                r[k, x + 1, t, rows, :] = out[i]
            elif cy == 1:
                v = pltpu.roll(out[i], 1, 1)
                r[k, x + 1, t, rows, 1:LANES] = v[:, 1:LANES]
                r[k, x + 1, lax.rem(t + 1, NT), rows, 0:1] = v[:, 0:1]
            else:
                v = pltpu.roll(out[i], LANES - 1, 1)
                r[k, x + 1, t, rows, 0:LANES - 1] = v[:, 0:LANES - 1]
                r[k, x + 1, lax.rem(t + 3, NT), rows, LANES - 1:LANES] = v[:, LANES - 1:LANES]
        B[0, x * NT + t] = out[16]
        B[1, x * NT + t] = out[17]

    def solid_at(x, t, z):
        return S[x, t, rows8(z), :] > 0

    def chunks(body):
        def step(n, _):
            z = 3 - n // NT
            t = lax.rem(n, NT)
            for x in range(2):
                body(x, t, z)
            return 0
        lax.fori_loop(0, 16, step, 0)

    def pull(e, x, t, z):
        f = []
        for i in range(19):
            cx, _, cz = VELOCITIES[i]
            f.append(R[e][SLOT[i], x + 1 - cx, t, pl.ds(8 + z * 8 - cz, 8), :])
        return f

    def forwards(e, side, dev, plane):
        return [
            remote(RB.at[e, k], R[e].at[5 * side + DIRECT + k, plane, :, 8:40, :], fw_s.at[e, k], xs_r.at[e, side, 1 + k], (dev, th))
            for k in range(2)
        ]

    def exchange(e):
        r = R[e]
        out = []
        for side, edge, dev, src, dst in ((0, last, right, 2, 0), (1, first, left, 1, 3)):
            pieces, via = [], []
            for k in range(2):
                slot = 5 * side + DIRECT + k
                pieces.append(remote(r.at[slot, src, :, 8:40, :], r.at[slot, dst, :, 8:40, :], xs_s.at[e, side, 1 + k], xs_r.at[e, side, 1 + k], (dev, th)))
                via.append(remote(r.at[slot, src, :, 8:40, :], RB.at[e, k], xs_s.at[e, side, 1 + k], rb_r.at[e, k], (opposite, th)))

            @pl.when(edge)
            def _():
                for c in via:
                    c.start()

            @pl.when(jnp.logical_not(edge))
            def _():
                for c in pieces:
                    c.start()

            straight = slice(5 * side, 5 * side + DIRECT)
            c = remote(r.at[straight, src, :, 8:40, :], r.at[straight, dst, :, 8:40, :], xs_s.at[e, side, 0], xs_r.at[e, side, 0], (dev, th))
            c.start()
            out += [c] + pieces
        for k in range(5):
            for x in range(2):
                for t in range(NT):
                    n = x * NT + t
                    ZU[e, k, n:n + 1, :] = r[SLOT[UP[k]], x + 1, t, 39:40, :]
                    ZD[e, k, n:n + 1, :] = r[SLOT[DOWN[k]], x + 1, t, 8:9, :]
        rims = [
            remote(ZU.at[e], RU.at[e, 0:5], zs_s.at[e, 0], zs_r.at[e, 0], (md, up)),
            remote(ZU.at[e, 3], RU.at[e, 5], zs_s.at[e, 1], zs_r.at[e, 1], (right, up)),
            remote(ZU.at[e, 4], RU.at[e, 6], zs_s.at[e, 2], zs_r.at[e, 2], (left, up)),
            remote(ZD.at[e], RD.at[e, 0:5], zs_s.at[e, 3], zs_r.at[e, 3], (md, dn)),
            remote(ZD.at[e, 4], RD.at[e, 5], zs_s.at[e, 4], zs_r.at[e, 4], (right, dn)),
            remote(ZD.at[e, 3], RD.at[e, 6], zs_s.at[e, 5], zs_r.at[e, 5], (left, dn)),
        ]
        for c in rims:
            c.start()

        @pl.when(first)
        def _():
            for k, c in enumerate(forwards(e, 0, ahead, 0)):
                remote(r.at[8 + k, 1, :, 8:40, :], RB.at[e, k], xs_s.at[e, 1, 1 + k], rb_r.at[e, k], (opposite, th)).wait_recv()
                c.start()

        @pl.when(last)
        def _():
            for k, c in enumerate(forwards(e, 1, behind, 3)):
                remote(r.at[3 + k, 2, :, 8:40, :], RB.at[e, k], xs_s.at[e, 0, 1 + k], rb_r.at[e, k], (opposite, th)).wait_recv()
                c.start()

        return out, rims

    def edges(e, sends):
        bulk, rims = sends
        for c in rims:
            c.wait_recv()
        low = sub < NT
        is_open = W[...] == 1
        for k in range(5):
            for vertical, pop in ((0, UP[k]), (1, DOWN[k])):
                src = RD if vertical else RU
                cx = VELOCITIES[pop][0]
                tile = src[e, k]
                if cx == 1:
                    tile = pltpu.roll(jnp.where(low, tile, src[e, 5]), NT, 0)
                elif cx == -1:
                    tile = pltpu.roll(jnp.where(low, src[e, 6], tile), NT, 0)
                if vertical:
                    tile = jnp.where(th == 3, WEIGHTS[pop] * INLET_DENSITY, tile)
                    row = 40
                else:
                    if VELOCITIES[pop][1] == 0:
                        wall = ZD[e, k]
                    else:
                        wall = jnp.concatenate([B[k - 1, n, 0:1, :] for n in range(8)], axis=0)
                    wall = jnp.where(is_open, WEIGHTS[pop] * OUTLET_DENSITY, wall)
                    tile = jnp.where(th == 0, wall, tile)
                    row = 7
                for x in range(2):
                    for t in range(NT):
                        n = x * NT + t
                        R[e][SLOT[pop], x + 1 - cx, t, row:row + 1, :] = tile[n:n + 1, :]
        for c in bulk:
            c.wait_recv()

    for t in range(NT):
        loads[5 + t].wait()

    def flow_first(x, t, z):
        put(0, x, t, z, collide([F[i, x, t, rows8(z), :] for i in range(19)], solid_at(x, t, z)))

    chunks(flow_first)
    sent0 = exchange(0)
    forward_fines(0)

    def inverse(s, _):
        d = jnp.full((8, LANES), diff[s], jnp.float32)
        h = 0.5 * lax.rsqrt(d)
        theta = -2.0 * jnp.log1p(h + h * h / (1.0 + jnp.sqrt(1.0 + h * h)))
        j = lane.astype(jnp.float32)
        full = 2.0 * LANES
        norm = 1.0 / (jnp.sqrt(4.0 * d + 1.0) * (1.0 - jnp.exp(theta * full)))
        for zc in range(16):
            i = (sub + zc * 8).astype(jnp.float32)
            gap = jnp.abs(i - j)
            away = i + j + 1.0
            g = jnp.exp(theta * gap) + jnp.exp(theta * (full - gap))
            g = g + (jnp.exp(theta * away) + jnp.exp(theta * (full - away)))
            G[zc * 8:zc * 8 + 8, :] = g * norm
        g = G[...]
        hi = g.astype(jnp.bfloat16)
        GB[s, :, 0:LANES] = hi
        GB[s, :, LANES:2 * LANES] = (g - hi.astype(jnp.float32)).astype(jnp.bfloat16)
        return 0

    lax.fori_loop(0, 4, inverse, 0)

    edges(0, sent0)

    def flow_second(x, t, z):
        put(1, x, t, z, collide(pull(0, x, t, z), solid_at(x, t, z)))

    chunks(flow_second)
    sent1 = exchange(1)
    edges(1, sent1)

    def flow_last(x, t, z):
        f = pull(1, x, t, z)
        rows = rows8(z)
        for i in range(19):
            pops_out[i, x, rows, pl.ds(pl.multiple_of(t * LANES, LANES), LANES)] = f[i]
        _, _, mass, flux = pair_moments(f)
        fluid = (1.0 - S[x, t, rows, :]) / mass
        for a in range(3):
            V[a, x, t, rows, :] = flux[a] * fluid

    chunks(flow_last)
    speeds = [
        remote(V.at[:, :, p], Vall.at[:, :, my_rows, :], vs_s.at[k], vs_r.at[k], (md, p))
        for k, p in enumerate(peers)
    ]
    for c in speeds:
        c.start()
    for a in range(3):
        for x in range(2):
            Vall[a, x, my_rows, :] = V[a, x, th]

    for c in solids:
        c.wait_recv()
    for c in speeds:
        c.wait_recv()

    def coefficients(n, _):
        for x in range(2):
            for m in range(4):
                rows = rows8(n * 4 + m)
                ux, uy, uz = [Vall[a, x, rows, :] for a in range(3)]
                C[0, x, rows, :] = (1.0 - 4.0 * LATERAL_DIFFUSION) - (jnp.abs(ux) + jnp.abs(uy) + jnp.abs(uz))
                C[1, x, rows, :] = LATERAL_DIFFUSION + jnp.maximum(ux, 0.0)
                C[2, x, rows, :] = LATERAL_DIFFUSION - jnp.minimum(ux, 0.0)
                C[3, x, rows, :] = LATERAL_DIFFUSION + jnp.maximum(uy, 0.0)
                C[4, x, rows, :] = LATERAL_DIFFUSION - jnp.minimum(uy, 0.0)
                C[5, x, rows, :] = jnp.maximum(uz, 0.0)
                C[6, x, rows, :] = -jnp.minimum(uz, 0.0)
        return 0

    lax.fori_loop(0, 4, coefficients, 0)

    def transport(step, s):
        q = Q[step]
        for x in range(2):
            q[s, x + 1, 7:8, :] = q[s, x + 1, 8:9, :]
            q[s, x + 1, 136:137, :] = q[s, x + 1, 135:136, :]
        for c in fine_copies(step, s):
            c.wait_recv()
        west_in = YW[step, s]
        east_in = YE[step, s]
        kept = ret[s]
        for x in range(2):
            for zc in range(16):
                n = x * 16 + zc
                rows = slice(zc * 8, zc * 8 + 8)
                held = slice(zc * 8 + 8, zc * 8 + 16)
                c = q[s, x + 1, held, :]
                below = q[s, x + 1, zc * 8 + 7:zc * 8 + 15, :]
                above = q[s, x + 1, zc * 8 + 9:zc * 8 + 17, :]
                from_west = pltpu.roll(west_in, LANES - n, 1) if n else west_in
                from_east = pltpu.roll(east_in, LANES - 1 - n, 1)
                south = jnp.where(lane == 0, from_west, pltpu.roll(c, 1, 1))
                north = jnp.where(lane == LANES - 1, from_east, pltpu.roll(c, LANES - 1, 1))
                X[rows, x * LANES:(x + 1) * LANES] = total([
                    c * (C[0, x, rows, :] - kept * Sall[x, rows, :]),
                    q[s, x, held, :] * C[1, x, rows, :],
                    q[s, x + 2, held, :] * C[2, x, rows, :],
                    south * C[3, x, rows, :],
                    north * C[4, x, rows, :],
                    below * C[5, x, rows, :],
                    above * C[6, x, rows, :],
                ])
        v = X[...]
        v_hi = v.astype(jnp.bfloat16)
        v_lo = (v - v_hi.astype(jnp.float32)).astype(jnp.bfloat16)
        out = jnp.dot(GB[s], jnp.concatenate([v_hi, v_hi], axis=0), preferred_element_type=jnp.float32)
        out += jnp.dot(GB[s, :, 0:LANES], v_lo, preferred_element_type=jnp.float32)
        for x in range(2):
            part = out[:, x * LANES:(x + 1) * LANES]
            if step == 0:
                Q1[s, x + 1, 8:136, :] = part
            else:
                fines_out[s, x] = part

    def transport_first(s, _):
        transport(0, s)
        pack_columns(1, s)
        start_fines(1, s)
        return 0

    lax.fori_loop(0, 4, transport_first, 0)
    forward_fines(1)

    def transport_second(s, _):
        transport(1, s)
        return 0

    lax.fori_loop(0, 4, transport_second, 0)

    for c in sent0[0] + sent0[1] + sent1[0] + sent1[1] + solids + speeds:
        c.wait_send()
    for step in range(2):
        for s in range(4):
            for c in fine_copies(step, s):
                c.wait_send()

    @pl.when(corner)
    def _():
        for e in range(2):
            for c in forwards(e, 0, ahead, 0) + fine_forwards(e, 0, ahead, 0):
                c.wait_send()


def on_device(populations, fibre_mask, wire_open, fines, diffusivity, retention):
    any_ = pl.BlockSpec(memory_space=pl.ANY)
    vmem = pl.BlockSpec(memory_space=pltpu.VMEM)
    f32 = jnp.float32
    dma = pltpu.SemaphoreType.DMA
    populations_out, fines_out = pl.pallas_call(
        kernel,
        out_shape=(
            jax.ShapeDtypeStruct(populations.shape, f32),
            jax.ShapeDtypeStruct(fines.shape, f32),
        ),
        in_specs=[any_] * 6,
        out_specs=(vmem, vmem),
        scratch_shapes=[
            pltpu.VMEM(wire_open.shape, jnp.int32),
            pltpu.SMEM(diffusivity.shape, f32),
            pltpu.SMEM(retention.shape, f32),
            pltpu.VMEM((19, 2, NT, 32, LANES), f32),
            pltpu.VMEM((19, 4, NT, 48, LANES), f32),
            pltpu.VMEM((19, 4, NT, 48, LANES), f32),
            pltpu.VMEM((2, NT, 32, LANES), jnp.int32),
            pltpu.VMEM((2, NT, 32, LANES), f32),
            pltpu.VMEM((2, 128, LANES), f32),
            pltpu.VMEM((3, 2, NT, 32, LANES), f32),
            pltpu.VMEM((3, 2, 128, LANES), f32),
            pltpu.VMEM((2, 8, 8, LANES), f32),
            pltpu.VMEM((2, 5, 8, LANES), f32),
            pltpu.VMEM((2, 5, 8, LANES), f32),
            pltpu.VMEM((2, 7, 8, LANES), f32),
            pltpu.VMEM((2, 7, 8, LANES), f32),
            pltpu.VMEM((8, LANES), jnp.int32),
            pltpu.VMEM((4, 4, 144, LANES), f32),
            pltpu.VMEM((4, 4, 144, LANES), f32),
            pltpu.VMEM((7, 2, 128, LANES), f32),
            pltpu.VMEM((128, 2 * LANES), f32),
            pltpu.VMEM((128, LANES), f32),
            pltpu.VMEM((4, 128, 2 * LANES), jnp.bfloat16),
            pltpu.VMEM((2, 4, 2, 8, LANES), f32),
            pltpu.VMEM((2, 4, 8, LANES), f32),
            pltpu.VMEM((2, 4, 8, LANES), f32),
            pltpu.VMEM((2, 2, NT, 32, LANES), f32),
            pltpu.VMEM((2, 2, 128, LANES), f32),
            dma((12,)),
            dma((2, 2, 3)), dma((2, 2, 3)),
            dma((2, 6)), dma((2, 6)),
            dma((3,)), dma((3,)),
            dma((3,)), dma((3,)),
            dma((2, 4, 2)), dma((2, 4, 2)),
            dma((2, 4, 2)), dma((2, 4, 2)),
            dma((2, 2)), dma((2, 2)),
            dma((2, 2)), dma((2, 2)),
        ],
        compiler_params=pltpu.CompilerParams(
            collective_id=0, has_side_effects=True, vmem_limit_bytes=48 * 1024 * 1024),
        name="drainage",
    )(*[
        pltpu.with_memory_space_constraint(v, pltpu.HBM)
        for v in (populations, fibre_mask, wire_open, fines, diffusivity, retention)
    ])
    return populations_out, fines_out


def solution(mesh):
    return jax.shard_map(
        on_device,
        mesh=mesh,
        in_specs=(
            P(None, "md", "th", None), P("md", "th", None), P("md", None),
            P(None, "md", None, "th"), P(), P(),
        ),
        out_specs=(P(None, "md", "th", None), P(None, "md", None, "th")),
        check_vma=False,
    )
```

```python
import functools

import jax
import jax.numpy as jnp
from jax import lax
from jax.experimental import pallas as pl
from jax.experimental.pallas import tpu as pltpu
from jax.sharding import PartitionSpec as P

VELOCITIES = [
    (0, 0, 0), (1, 0, 0), (-1, 0, 0), (0, 1, 0), (0, -1, 0), (0, 0, 1), (0, 0, -1),
    (1, 1, 0), (-1, -1, 0), (1, -1, 0), (-1, 1, 0), (1, 0, 1), (-1, 0, -1), (1, 0, -1),
    (-1, 0, 1), (0, 1, 1), (0, -1, -1), (0, 1, -1), (0, -1, 1),
]
WEIGHTS = [1.0 / 3.0] + [1.0 / 18.0] * 6 + [1.0 / 36.0] * 12
OPPOSITE = [0, 2, 1, 4, 3, 6, 5, 8, 7, 10, 9, 12, 11, 14, 13, 16, 15, 18, 17]
RELAXATION = 1.6
INLET_DENSITY = 1.03
OUTLET_DENSITY = 0.97
LATERAL_DIFFUSION = 0.1

PLUS = [1, 7, 9, 11, 13]
MINUS = [2, 8, 10, 12, 14]
ZERO = [0, 3, 4, 5, 6, 15, 16, 17, 18]
SLOT = {i: k for k, i in enumerate(PLUS + MINUS + ZERO)}
UP = [5, 15, 18, 11, 14]
DOWN = [6, 16, 17, 12, 13]

MESH = pl.DeviceIdType.MESH
LANES = 128
NT = 4
TOP = 8


def total(items):
    items = list(items)
    while len(items) > 1:
        items = [a + b for a, b in zip(items[::2], items[1::2])] + (
            [items[-1]] if len(items) % 2 else []
        )
    return items[0]


PAIRS = list(range(1, 19, 2))


def signed(terms):
    plus = [v for c, v in terms if c > 0]
    minus = [v for c, v in terms if c < 0]
    return total(plus) - total(minus) if minus else total(plus)


def pair_moments(f):
    even = {i: f[i] + f[i + 1] for i in PAIRS}
    odd = {i: f[i] - f[i + 1] for i in PAIRS}
    mass = total([f[0]] + [even[i] for i in PAIRS])
    flux = [
        signed([(VELOCITIES[i][a], odd[i]) for i in PAIRS if VELOCITIES[i][a]]) for a in range(3)
    ]
    return even, odd, mass, flux


def collide(f, solid):
    even, odd, mass, flux = pair_moments(f)
    scale = (4.5 ** 0.5) / mass
    px, py, pz = [v * scale for v in flux]
    base = 1.0 - (1.0 / 3.0) * (px * px + py * py + pz * pz)
    keep = 1.0 - RELAXATION
    k_even = jnp.where(solid, 0.5, 0.5 * keep)
    k_odd = jnp.where(solid, -0.5, 0.5 * keep)
    m_diag = jnp.where(solid, 0.0, (RELAXATION * WEIGHTS[7]) * mass)
    m_axis = m_diag + m_diag
    odd_diag, odd_axis = (2.0 ** 0.5) * m_diag, (2.0 ** 0.5) * m_axis
    out = [None] * 19
    out[0] = jnp.where(solid, 1.0, keep) * f[0] + (WEIGHTS[0] / WEIGHTS[7]) * (m_diag * base)
    for i in PAIRS:
        p = signed([(c, v) for c, v in zip(VELOCITIES[i], (px, py, pz)) if c])
        axis = i < 7
        a = k_even * even[i] + (m_axis if axis else m_diag) * (base + p * p)
        b = k_odd * odd[i] + (odd_axis if axis else odd_diag) * p
        out[i] = a + b
        out[i + 1] = a - b
    return out


QUARTERS = (3, 2, 1, 0)
WAYS = {3: 0, 2: 1, 1: None, 0: None}
RELAYED = 2


def kernel(
    pops, mask, wire_hbm, fines, diff_hbm, ret_hbm, pops_out, fines_out,
    wire, diff, ret, F, R0, R1, M, S, Sall, V, Vall, B, ZU, ZD, RU, RD, W, Q0, Q1, C, X, G, GB, YP, YW, YE, RB, QB,
    in_sem, xs_s, xs_r, zs_s, zs_r, ss_s, ss_r, vs_s, vs_r, q_s, q_r, y_s, y_r,
    rb_r, fw_s, qb_r, qf_s,
):
    md = lax.axis_index("md")
    th = lax.axis_index("th")
    nmd = lax.axis_size("md")
    right, left = lax.rem(md + 1, nmd), lax.rem(md + nmd - 1, nmd)
    up, dn = lax.rem(th + 1, 4), lax.rem(th + 3, 4)
    peers = [lax.rem(th + d, 4) for d in (1, 2, 3)]
    R = (R0, R1)
    Q = (Q0, Q1)
    place = lax.rem(md, 16)
    base = md - place
    spot = {p: lax.rem(base + p, nmd) for p in (0, 3, 12, 15)}
    ahead, behind = lax.rem(base + 16, nmd), lax.rem(base + nmd - 1, nmd)
    by_way = ((spot[0], spot[3], spot[12]), (spot[15], spot[12], spot[3]))
    source = (place == 15, place == 0)
    is_relay = ((place == 0) | (place == 3) | (place == 12), (place == 15) | (place == 3) | (place == 12))
    part = (
        jnp.where(place == 0, 0, jnp.where(place == 3, 1, 2)),
        jnp.where(place == 15, 0, jnp.where(place == 12, 1, 2)),
    )
    quarter_of = [jnp.where(p == 0, 3, jnp.where(p == 1, 2, 0)) for p in part]
    species_of = [jnp.where(p == 0, 0, jnp.where(p == 1, 1, 0)) for p in part]
    relays_flow = [is_relay[side] & ((part[side] == 0) | (part[side] == 1)) for side in range(2)]
    relays_fines = [is_relay[side] & ((part[side] == 0) | (part[side] == 1)) for side in range(2)]
    target = (ahead, behind)
    came_from = (spot[15], spot[0])

    loads = [
        pltpu.make_async_copy(fines, Q0.at[:, 1:3, 8:136, :], in_sem.at[0]),
    ]
    loads.append(pltpu.make_async_copy(mask, M, in_sem.at[1]))
    for z in QUARTERS:
        loads.append(pltpu.make_async_copy(
            pops.at[:, :, z * 8:z * 8 + 8, :], F.at[:, :, z * 8:z * 8 + 8, :], in_sem.at[2 + z]))
    small = [
        pltpu.make_async_copy(a, b, in_sem.at[6 + k])
        for k, (a, b) in enumerate(((wire_hbm, wire), (diff_hbm, diff), (ret_hbm, ret)))
    ]
    for c in loads + small:
        c.start()

    barrier = pltpu.get_barrier_semaphore()
    friends = [(right, th), (left, th)] + [(md, p) for p in peers]
    friends += [(m, t) for m in (right, left) for t in (up, dn)]
    for d in friends:
        pl.semaphore_signal(barrier, inc=1, device_id=d, device_id_type=MESH)

    more = {
        0: [spot[15], spot[12], spot[3], ahead] + [lax.rem(base + nmd - 16 + p, nmd) for p in (0, 3, 12)],
        15: [spot[0], spot[3], spot[12], behind] + [lax.rem(base + 16 + p, nmd) for p in (15, 12, 3)],
        3: [spot[15], spot[0], ahead, behind],
        12: [spot[15], spot[0], ahead, behind],
    }
    for p in more:
        @pl.when(place == p)
        def _(p=p):
            for m in more[p]:
                pl.semaphore_signal(barrier, inc=1, device_id=(m, th), device_id_type=MESH)

    lane = lax.broadcasted_iota(jnp.int32, (8, LANES), 1)
    sub = lax.broadcasted_iota(jnp.int32, (8, LANES), 0)

    def remote(src, dst, s, r, dev):
        return pltpu.make_async_remote_copy(
            src_ref=src, dst_ref=dst, send_sem=s, recv_sem=r, device_id=dev, device_id_type=MESH)

    def rows8(z):
        return pl.ds(pl.multiple_of(z * 8, 8), 8)

    def pack_columns(step, s):
        east = west = jnp.zeros((8, LANES), jnp.float32)
        for x in range(2):
            for zc in range(16):
                k = x * 16 + zc
                c = Q[step][s, x + 1, 8 + zc * 8:16 + zc * 8, :]
                east = jnp.where(lane == k, pltpu.roll(c, k + 1, 1), east)
                west = jnp.where(lane == k, pltpu.roll(c, k, 1) if k else c, west)
        YP[step, s, 0] = east
        YP[step, s, 1] = west

    def fine_copies(step, s):
        q = Q[step]
        return [
            remote(q.at[s, 2, 8:136, :], q.at[s, 0, 8:136, :], q_s.at[step, s, 0], q_r.at[step, s, 0], (right, th)),
            remote(q.at[s, 1, 8:136, :], q.at[s, 3, 8:136, :], q_s.at[step, s, 1], q_r.at[step, s, 1], (left, th)),
            remote(YP.at[step, s, 0], YW.at[step, s], y_s.at[step, s, 0], y_r.at[step, s, 0], (md, up)),
            remote(YP.at[step, s, 1], YE.at[step, s], y_s.at[step, s, 1], y_r.at[step, s, 1], (md, dn)),
        ]

    def start_rows(step, s):
        for c in fine_copies(step, s)[2:]:
            c.start()

    def start_planes(step, s):
        q = Q[step]
        copies = fine_copies(step, s)
        for side, plane in ((0, 2), (1, 1)):
            a, b, c = [by_way[side][w] for w in (0, 1, 1)]
            via = source[side] & (s < RELAYED)
            dev = jnp.where(s == 0, a, jnp.where(s == 1, b, c))

            @pl.when(via)
            def _():
                remote(q.at[s, plane, 8:136, :], QB.at[step, side], q_s.at[step, s, side], qb_r.at[step, side], (dev, th)).start()

            @pl.when(jnp.logical_not(via))
            def _():
                copies[side].start()

    def fine_forward(step, side):
        k = species_of[side]
        return remote(QB.at[step, side], Q[step].at[k, 3 * side, 8:136, :], qf_s.at[step, side], q_r.at[step, k, side], (target[side], th))

    def forward_fines(step):
        for side in range(2):
            @pl.when(relays_fines[side])
            def _():
                remote(Q[step].at[0, 1, 8:136, :], QB.at[step, side], qf_s.at[step, side], qb_r.at[step, side], (came_from[side], th)).wait_recv()
                fine_forward(step, side).start()

    loads[1].wait()
    for t in range(NT):
        S[:, t] = M[:, :, t * LANES:(t + 1) * LANES].astype(jnp.float32)

    my_rows = pl.ds(pl.multiple_of(th * 32, 32), 32)
    for x in range(2):
        Sall[x, my_rows, :] = S[x, th]

    def put(e, x, t, z, out):
        rows = slice(8 + z * 8, 16 + z * 8)
        r = R[e]
        for i in range(19):
            cy = VELOCITIES[i][1]
            k = SLOT[i]
            if cy == 0:
                r[k, x + 1, t, rows, :] = out[i]
            elif cy == 1:
                v = pltpu.roll(out[i], 1, 1)
                r[k, x + 1, t, rows, 1:LANES] = v[:, 1:LANES]
                r[k, x + 1, lax.rem(t + 1, NT), rows, 0:1] = v[:, 0:1]
            else:
                v = pltpu.roll(out[i], LANES - 1, 1)
                r[k, x + 1, t, rows, 0:LANES - 1] = v[:, 0:LANES - 1]
                r[k, x + 1, lax.rem(t + 3, NT), rows, LANES - 1:LANES] = v[:, LANES - 1:LANES]
        if z == 0:
            B[0, x * NT + t] = out[16]
            B[1, x * NT + t] = out[17]

    def solid_at(x, t, z):
        return S[x, t, z * 8:z * 8 + 8, :] > 0

    def chunks(z, body):
        def step(t, _):
            for x in range(2):
                body(x, t, z)
            return 0
        lax.fori_loop(0, NT, step, 0)

    def tile(t):
        return pl.ds(pl.multiple_of(t * LANES, LANES), LANES)

    def pull(e, x, t, z):
        f = []
        for i in range(19):
            cx, _, cz = VELOCITIES[i]
            f.append(R[e][SLOT[i], x + 1 - cx, t, 8 + z * 8 - cz:16 + z * 8 - cz, :])
        return f

    def quarter(e, side, z):
        r = R[e]
        rows = slice(8 + z * 8, 16 + z * 8)
        slots = slice(5 * side, 5 * side + 5)
        return remote(
            r.at[slots, 2 - side, :, rows, :], r.at[slots, 3 * side, :, rows, :],
            xs_s.at[e, side, z], xs_r.at[e, side, z], ((right, left)[side], th))

    def rim_copies(e):
        return [
            remote(ZU.at[e], RU.at[e, 0:5], zs_s.at[e, 0], zs_r.at[e, 0], (md, up)),
            remote(ZU.at[e, 3], RU.at[e, 5], zs_s.at[e, 1], zs_r.at[e, 1], (right, up)),
            remote(ZU.at[e, 4], RU.at[e, 6], zs_s.at[e, 2], zs_r.at[e, 2], (left, up)),
            remote(ZD.at[e], RD.at[e, 0:5], zs_s.at[e, 3], zs_r.at[e, 3], (md, dn)),
            remote(ZD.at[e, 4], RD.at[e, 5], zs_s.at[e, 4], zs_r.at[e, 4], (right, dn)),
            remote(ZD.at[e, 3], RD.at[e, 6], zs_s.at[e, 5], zs_r.at[e, 5], (left, dn)),
        ]

    def send(e, z):
        r = R[e]
        if z in (3, 0):
            pack, list_, row = (ZU, UP, 39) if z == 3 else (ZD, DOWN, 8)
            for k in range(5):
                for x in range(2):
                    for t in range(NT):
                        n = x * NT + t
                        pack[e, k, n:n + 1, :] = r[SLOT[list_[k]], x + 1, t, row:row + 1, :]
            for c in rim_copies(e)[0 if z == 3 else 3:][:3]:
                c.start()
        rows = slice(8 + z * 8, 16 + z * 8)
        for side in range(2):
            c = quarter(e, side, z)
            if WAYS[z] is None:
                c.start()
                continue

            @pl.when(source[side])
            def _():
                slots = slice(5 * side, 5 * side + 5)
                remote(r.at[slots, 2 - side, :, rows, :], RB.at[e, side], xs_s.at[e, side, z], rb_r.at[e, side], (by_way[side][WAYS[z]], th)).start()

            @pl.when(jnp.logical_not(source[side]))
            def _():
                c.start()

    def forward(e, side):
        z = quarter_of[side]
        rows = pl.ds(pl.multiple_of(8 + z * 8, 8), 8)
        slots = slice(5 * side, 5 * side + 5)
        return remote(RB.at[e, side], R[e].at[slots, 3 * side, :, rows, :], fw_s.at[e, side], xs_r.at[e, side, z], (target[side], th))

    def relay(e):
        for side in range(2):
            @pl.when(relays_flow[side])
            def _():
                slots = slice(5 * side, 5 * side + 5)
                remote(R[e].at[slots, 2 - side, :, 8:16, :], RB.at[e, side], fw_s.at[e, side], rb_r.at[e, side], (came_from[side], th)).wait_recv()
                forward(e, side).start()

    def rims(e, vertical):
        for c in rim_copies(e)[3 * vertical:3 * vertical + 3]:
            c.wait_recv()
        low = sub < NT
        is_open = W[...] == 1
        src = RD if vertical else RU
        for k in range(5):
            pop = DOWN[k] if vertical else UP[k]
            cx = VELOCITIES[pop][0]
            rim = src[e, k]
            if cx == 1:
                rim = pltpu.roll(jnp.where(low, rim, src[e, 5]), NT, 0)
            elif cx == -1:
                rim = pltpu.roll(jnp.where(low, src[e, 6], rim), NT, 0)
            if vertical:
                rim = jnp.where(th == 3, WEIGHTS[pop] * INLET_DENSITY, rim)
                row = 40
            else:
                if VELOCITIES[pop][1] == 0:
                    wall = ZD[e, k]
                else:
                    wall = jnp.concatenate([B[k - 1, n, 0:1, :] for n in range(8)], axis=0)
                wall = jnp.where(is_open, WEIGHTS[pop] * OUTLET_DENSITY, wall)
                rim = jnp.where(th == 0, wall, rim)
                row = 7
            for x in range(2):
                for t in range(NT):
                    n = x * NT + t
                    R[e][SLOT[pop], x + 1 - cx, t, row:row + 1, :] = rim[n:n + 1, :]

    def arrive(e, z):
        if z == 3:
            quarter(e, 0, 3).wait_recv()
            quarter(e, 1, 3).wait_recv()
            rims(e, 1)
        if z > 0:
            quarter(e, 0, z - 1).wait_recv()
            quarter(e, 1, z - 1).wait_recv()
        else:
            rims(e, 0)

    def await_friends():
        @pl.when(source[0] | source[1])
        def _():
            pl.semaphore_wait(barrier, len(friends) + 7)

        @pl.when((place == 3) | (place == 12))
        def _():
            pl.semaphore_wait(barrier, len(friends) + 4)

        @pl.when(jnp.logical_not(is_relay[0] | is_relay[1]))
        def _():
            pl.semaphore_wait(barrier, len(friends))

    def flow_first(x, t, z):
        rows = slice(z * 8, z * 8 + 8)
        put(0, x, t, z, collide([F[i, x, rows, tile(t)] for i in range(19)], solid_at(x, t, z)))

    solids = [
        remote(S.at[:, p], Sall.at[:, my_rows, :], ss_s.at[k], ss_r.at[k], (md, p))
        for k, p in enumerate(peers)
    ]
    def planes(s, _):
        start_planes(0, s)
        return 0

    for z in QUARTERS:
        loads[2 + QUARTERS.index(z)].wait()
        chunks(z, flow_first)
        if z == 3:
            await_friends()
        send(0, z)
    loads[0].wait()
    lax.fori_loop(0, 4, planes, 0)
    relay(0)
    forward_fines(0)

    def pack_first(s, _):
        pack_columns(0, s)
        return 0

    lax.fori_loop(0, 4, pack_first, 0)

    def send_rows(s, _):
        start_rows(0, s)
        return 0

    lax.fori_loop(0, 4, send_rows, 0)
    for c in solids:
        c.start()
    for c in small:
        c.wait()
    for x in range(2):
        for t in range(NT):
            W[x * NT + t:x * NT + t + 1, :] = wire[x:x + 1, t * LANES:(t + 1) * LANES]


    def inverse(s, _):
        d = jnp.full((8, LANES), diff[s], jnp.float32)
        h = 0.5 * lax.rsqrt(d)
        theta = -2.0 * jnp.log1p(h + h * h / (1.0 + jnp.sqrt(1.0 + h * h)))
        j = lane.astype(jnp.float32)
        full = 2.0 * LANES
        norm = 1.0 / (jnp.sqrt(4.0 * d + 1.0) * (1.0 - jnp.exp(theta * full)))
        for zc in range(16):
            i = (sub + zc * 8).astype(jnp.float32)
            gap = jnp.abs(i - j)
            away = i + j + 1.0
            g = jnp.exp(theta * gap) + jnp.exp(theta * (full - gap))
            g = g + (jnp.exp(theta * away) + jnp.exp(theta * (full - away)))
            G[zc * 8:zc * 8 + 8, :] = g * norm
        g = G[...]
        hi = g.astype(jnp.bfloat16)
        GB[s, :, 0:LANES] = hi
        GB[s, :, LANES:2 * LANES] = (g - hi.astype(jnp.float32)).astype(jnp.bfloat16)
        return 0

    lax.fori_loop(0, 4, inverse, 0)

    def flow_second(x, t, z):
        put(1, x, t, z, collide(pull(0, x, t, z), solid_at(x, t, z)))

    for z in QUARTERS:
        arrive(0, z)
        chunks(z, flow_second)
        send(1, z)

    relay(1)

    def flow_last(x, t, z):
        f = pull(1, x, t, z)
        rows = slice(z * 8, z * 8 + 8)
        for i in range(19):
            pops_out[i, x, rows, tile(t)] = f[i]
        _, _, mass, flux = pair_moments(f)
        fluid = (1.0 - S[x, t, rows, :]) / mass
        for a in range(3):
            V[a, x, t, rows, :] = flux[a] * fluid

    def speeds(z):
        there = pl.ds(pl.multiple_of(th * 32 + z * 8, 8), 8)
        return [
            remote(V.at[:, :, p, z * 8:z * 8 + 8, :], Vall.at[:, :, there, :], vs_s.at[k, z], vs_r.at[k, z], (md, p))
            for k, p in enumerate(peers)
        ]

    for z in QUARTERS:
        arrive(1, z)
        chunks(z, flow_last)
        for c in speeds(z):
            c.start()
    for a in range(3):
        for x in range(2):
            Vall[a, x, my_rows, :] = V[a, x, th]

    for c in solids:
        c.wait_recv()
    for z in QUARTERS:
        for c in speeds(z):
            c.wait_recv()

    def coefficients(n, _):
        for x in range(2):
            for m in range(4):
                rows = rows8(n * 4 + m)
                ux, uy, uz = [Vall[a, x, rows, :] for a in range(3)]
                C[0, x, rows, :] = (1.0 - 4.0 * LATERAL_DIFFUSION) - (jnp.abs(ux) + jnp.abs(uy) + jnp.abs(uz))
                C[1, x, rows, :] = LATERAL_DIFFUSION + jnp.maximum(ux, 0.0)
                C[2, x, rows, :] = LATERAL_DIFFUSION - jnp.minimum(ux, 0.0)
                C[3, x, rows, :] = LATERAL_DIFFUSION + jnp.maximum(uy, 0.0)
                C[4, x, rows, :] = LATERAL_DIFFUSION - jnp.minimum(uy, 0.0)
                C[5, x, rows, :] = jnp.maximum(uz, 0.0)
                C[6, x, rows, :] = -jnp.minimum(uz, 0.0)
        return 0

    lax.fori_loop(0, 4, coefficients, 0)

    def transport(step, s):
        q = Q[step]
        for x in range(2):
            q[s, x + 1, 7:8, :] = q[s, x + 1, 8:9, :]
            q[s, x + 1, 136:137, :] = q[s, x + 1, 135:136, :]
        for c in fine_copies(step, s):
            c.wait_recv()
        west_in = YW[step, s]
        east_in = YE[step, s]
        kept = ret[s]
        for x in range(2):
            for zc in range(16):
                n = x * 16 + zc
                rows = slice(zc * 8, zc * 8 + 8)
                held = slice(zc * 8 + 8, zc * 8 + 16)
                c = q[s, x + 1, held, :]
                below = q[s, x + 1, zc * 8 + 7:zc * 8 + 15, :]
                above = q[s, x + 1, zc * 8 + 9:zc * 8 + 17, :]
                from_west = pltpu.roll(west_in, LANES - n, 1) if n else west_in
                from_east = pltpu.roll(east_in, LANES - 1 - n, 1)
                south = jnp.where(lane == 0, from_west, pltpu.roll(c, 1, 1))
                north = jnp.where(lane == LANES - 1, from_east, pltpu.roll(c, LANES - 1, 1))
                X[rows, x * LANES:(x + 1) * LANES] = total([
                    c * (C[0, x, rows, :] - kept * Sall[x, rows, :]),
                    q[s, x, held, :] * C[1, x, rows, :],
                    q[s, x + 2, held, :] * C[2, x, rows, :],
                    south * C[3, x, rows, :],
                    north * C[4, x, rows, :],
                    below * C[5, x, rows, :],
                    above * C[6, x, rows, :],
                ])
        v = X[...]
        v_hi = v.astype(jnp.bfloat16)
        v_lo = (v - v_hi.astype(jnp.float32)).astype(jnp.bfloat16)
        out = jnp.dot(GB[s], jnp.concatenate([v_hi, v_hi], axis=0), preferred_element_type=jnp.float32)
        out += jnp.dot(GB[s, :, 0:LANES], v_lo, preferred_element_type=jnp.float32)
        for x in range(2):
            part = out[:, x * LANES:(x + 1) * LANES]
            if step == 0:
                Q1[s, x + 1, 8:136, :] = part
            else:
                fines_out[s, x] = part

    def transport_first(s, _):
        transport(0, s)
        pack_columns(1, s)
        start_rows(1, s)
        start_planes(1, s)
        return 0

    lax.fori_loop(0, 4, transport_first, 0)
    forward_fines(1)

    def transport_second(s, _):
        transport(1, s)
        return 0

    lax.fori_loop(0, 4, transport_second, 0)

    for c in solids:
        c.wait_send()
    for z in QUARTERS:
        for c in speeds(z):
            c.wait_send()
        for e in range(2):
            for side in range(2):
                quarter(e, side, z).wait_send()
    for step in range(2):
        for c in rim_copies(step):
            c.wait_send()
        for s in range(4):
            for c in fine_copies(step, s):
                c.wait_send()
        for side in range(2):
            @pl.when(relays_flow[side])
            def _():
                forward(step, side).wait_send()

            @pl.when(relays_fines[side])
            def _():
                fine_forward(step, side).wait_send()


def on_device(populations, fibre_mask, wire_open, fines, diffusivity, retention):
    any_ = pl.BlockSpec(memory_space=pl.ANY)
    vmem = pl.BlockSpec(memory_space=pltpu.VMEM)
    f32 = jnp.float32
    dma = pltpu.SemaphoreType.DMA
    populations_out, fines_out = pl.pallas_call(
        kernel,
        out_shape=(
            jax.ShapeDtypeStruct(populations.shape, f32),
            jax.ShapeDtypeStruct(fines.shape, f32),
        ),
        in_specs=[any_] * 6,
        out_specs=(vmem, vmem),
        scratch_shapes=[
            pltpu.VMEM(wire_open.shape, jnp.int32),
            pltpu.SMEM(diffusivity.shape, f32),
            pltpu.SMEM(retention.shape, f32),
            pltpu.VMEM(populations.shape, f32),
            pltpu.VMEM((19, 4, NT, 48, LANES), f32),
            pltpu.VMEM((19, 4, NT, 48, LANES), f32),
            pltpu.VMEM(fibre_mask.shape, jnp.int32),
            pltpu.VMEM((2, NT, 32, LANES), f32),
            pltpu.VMEM((2, 128, LANES), f32),
            pltpu.VMEM((3, 2, NT, 32, LANES), f32),
            pltpu.VMEM((3, 2, 128, LANES), f32),
            pltpu.VMEM((2, 8, 8, LANES), f32),
            pltpu.VMEM((2, 5, 8, LANES), f32),
            pltpu.VMEM((2, 5, 8, LANES), f32),
            pltpu.VMEM((2, 7, 8, LANES), f32),
            pltpu.VMEM((2, 7, 8, LANES), f32),
            pltpu.VMEM((8, LANES), jnp.int32),
            pltpu.VMEM((4, 4, 144, LANES), f32),
            pltpu.VMEM((4, 4, 144, LANES), f32),
            pltpu.VMEM((7, 2, 128, LANES), f32),
            pltpu.VMEM((128, 2 * LANES), f32),
            pltpu.VMEM((128, LANES), f32),
            pltpu.VMEM((4, 128, 2 * LANES), jnp.bfloat16),
            pltpu.VMEM((2, 4, 2, 8, LANES), f32),
            pltpu.VMEM((2, 4, 8, LANES), f32),
            pltpu.VMEM((2, 4, 8, LANES), f32),
            pltpu.VMEM((2, 2, 5, NT, 8, LANES), f32),
            pltpu.VMEM((2, 2, 128, LANES), f32),
            dma((9,)),
            dma((2, 2, 4)), dma((2, 2, 4)),
            dma((2, 6)), dma((2, 6)),
            dma((3,)), dma((3,)),
            dma((3, 4)), dma((3, 4)),
            dma((2, 4, 2)), dma((2, 4, 2)),
            dma((2, 4, 2)), dma((2, 4, 2)),
            dma((2, 2)), dma((2, 2)),
            dma((2, 2)), dma((2, 2)),
        ],
        compiler_params=pltpu.CompilerParams(
            collective_id=0, has_side_effects=True, vmem_limit_bytes=48 * 1024 * 1024),
        name="drainage",
    )(*[
        pltpu.with_memory_space_constraint(v, pltpu.HBM)
        for v in (populations, fibre_mask, wire_open, fines, diffusivity, retention)
    ])
    return populations_out, fines_out


def solution(mesh):
    return jax.shard_map(
        on_device,
        mesh=mesh,
        in_specs=(
            P(None, "md", "th", None), P("md", "th", None), P("md", None),
            P(None, "md", None, "th"), P(), P(),
        ),
        out_specs=(P(None, "md", "th", None), P(None, "md", None, "th")),
        check_vma=False,
    )
```

```python
import functools

import jax
import jax.numpy as jnp
from jax import lax
from jax.experimental import pallas as pl
from jax.experimental.pallas import tpu as pltpu
from jax.sharding import PartitionSpec as P

VELOCITIES = [
    (0, 0, 0), (1, 0, 0), (-1, 0, 0), (0, 1, 0), (0, -1, 0), (0, 0, 1), (0, 0, -1),
    (1, 1, 0), (-1, -1, 0), (1, -1, 0), (-1, 1, 0), (1, 0, 1), (-1, 0, -1), (1, 0, -1),
    (-1, 0, 1), (0, 1, 1), (0, -1, -1), (0, 1, -1), (0, -1, 1),
]
WEIGHTS = [1.0 / 3.0] + [1.0 / 18.0] * 6 + [1.0 / 36.0] * 12
OPPOSITE = [0, 2, 1, 4, 3, 6, 5, 8, 7, 10, 9, 12, 11, 14, 13, 16, 15, 18, 17]
RELAXATION = 1.6
INLET_DENSITY = 1.03
OUTLET_DENSITY = 0.97
LATERAL_DIFFUSION = 0.1

PLUS = [1, 7, 9, 11, 13]
MINUS = [2, 8, 10, 12, 14]
ZERO = [0, 3, 4, 5, 6, 15, 16, 17, 18]
SLOT = {i: k for k, i in enumerate(PLUS + MINUS + ZERO)}
UP = [5, 15, 18, 11, 14]
DOWN = [6, 16, 17, 12, 13]

MESH = pl.DeviceIdType.MESH
LANES = 128
NT = 4
TOP = 8


def total(items):
    items = list(items)
    while len(items) > 1:
        items = [a + b for a, b in zip(items[::2], items[1::2])] + (
            [items[-1]] if len(items) % 2 else []
        )
    return items[0]


PAIRS = list(range(1, 19, 2))


def signed(terms):
    plus = [v for c, v in terms if c > 0]
    minus = [v for c, v in terms if c < 0]
    return total(plus) - total(minus) if minus else total(plus)


def pair_moments(f):
    even = {i: f[i] + f[i + 1] for i in PAIRS}
    odd = {i: f[i] - f[i + 1] for i in PAIRS}
    mass = total([f[0]] + [even[i] for i in PAIRS])
    flux = [
        signed([(VELOCITIES[i][a], odd[i]) for i in PAIRS if VELOCITIES[i][a]]) for a in range(3)
    ]
    return even, odd, mass, flux


def collide(f, solid):
    even, odd, mass, flux = pair_moments(f)
    scale = (4.5 ** 0.5) / mass
    px, py, pz = [v * scale for v in flux]
    base = 1.0 - (1.0 / 3.0) * (px * px + py * py + pz * pz)
    keep = 1.0 - RELAXATION
    k_even = jnp.where(solid, 0.5, 0.5 * keep)
    k_odd = jnp.where(solid, -0.5, 0.5 * keep)
    m_diag = jnp.where(solid, 0.0, (RELAXATION * WEIGHTS[7]) * mass)
    m_axis = m_diag + m_diag
    odd_diag, odd_axis = (2.0 ** 0.5) * m_diag, (2.0 ** 0.5) * m_axis
    out = [None] * 19
    out[0] = jnp.where(solid, 1.0, keep) * f[0] + (WEIGHTS[0] / WEIGHTS[7]) * (m_diag * base)
    for i in PAIRS:
        p = signed([(c, v) for c, v in zip(VELOCITIES[i], (px, py, pz)) if c])
        axis = i < 7
        a = k_even * even[i] + (m_axis if axis else m_diag) * (base + p * p)
        b = k_odd * odd[i] + (odd_axis if axis else odd_diag) * p
        out[i] = a + b
        out[i + 1] = a - b
    return out


QUARTERS = (3, 2, 1, 0)
WAYS = {3: 0, 2: 1, 1: None, 0: None}
RELAYED = 2


def kernel(
    pops, mask, wire_hbm, fines, diff_hbm, ret_hbm, pops_out, fines_out,
    wire, diff, ret, F, R0, R1, M, S, Sall, V, Vall, B, ZU, ZD, RU, RD, W, Q0, Q1, C, X, G, GB, YP, YW, YE, RB, QB,
    in_sem, xs_s, xs_r, zs_s, zs_r, ss_s, ss_r, vs_s, vs_r, q_s, q_r, y_s, y_r,
    rb_r, fw_s, qb_r, qf_s,
):
    md = lax.axis_index("md")
    th = lax.axis_index("th")
    nmd = lax.axis_size("md")
    right, left = lax.rem(md + 1, nmd), lax.rem(md + nmd - 1, nmd)
    up, dn = lax.rem(th + 1, 4), lax.rem(th + 3, 4)
    peers = [lax.rem(th + d, 4) for d in (1, 2, 3)]
    R = (R0, R1)
    Q = (Q0, Q1)
    place = lax.rem(md, 16)
    base = md - place
    spot = {p: lax.rem(base + p, nmd) for p in (0, 3, 12, 15)}
    ahead, behind = lax.rem(base + 16, nmd), lax.rem(base + nmd - 1, nmd)
    by_way = ((spot[0], spot[3]), (spot[15], spot[12]))
    source = (place == 15, place == 0)
    is_relay = ((place == 0) | (place == 3), (place == 15) | (place == 12))
    part = (
        jnp.where(place == 0, 0, jnp.where(place == 3, 1, 2)),
        jnp.where(place == 15, 0, jnp.where(place == 12, 1, 2)),
    )
    quarter_of = [jnp.where(p == 0, 3, jnp.where(p == 1, 2, 0)) for p in part]
    species_of = [jnp.where(p == 0, 0, jnp.where(p == 1, 1, 0)) for p in part]
    relays_flow = [is_relay[side] & ((part[side] == 0) | (part[side] == 1)) for side in range(2)]
    relays_fines = [is_relay[side] & ((part[side] == 0) | (part[side] == 1)) for side in range(2)]
    target = (ahead, behind)
    came_from = (spot[15], spot[0])

    loads = [
        pltpu.make_async_copy(fines, Q0.at[:, 1:3, 8:136, :], in_sem.at[0]),
    ]
    loads.append(pltpu.make_async_copy(mask, M, in_sem.at[1]))
    for z in QUARTERS:
        loads.append(pltpu.make_async_copy(
            pops.at[:, :, z * 8:z * 8 + 8, :], F.at[:, :, z * 8:z * 8 + 8, :], in_sem.at[2 + z]))
    small = [
        pltpu.make_async_copy(a, b, in_sem.at[6 + k])
        for k, (a, b) in enumerate(((wire_hbm, wire), (diff_hbm, diff), (ret_hbm, ret)))
    ]
    for c in loads + small:
        c.start()

    barrier = pltpu.get_barrier_semaphore()
    friends = [(right, th), (left, th)] + [(md, p) for p in peers]
    friends += [(m, t) for m in (right, left) for t in (up, dn)]
    for d in friends:
        pl.semaphore_signal(barrier, inc=1, device_id=d, device_id_type=MESH)

    more = {
        0: [spot[15], spot[12], ahead] + [lax.rem(base + nmd - 16 + p, nmd) for p in (0, 3)],
        15: [spot[0], spot[3], behind] + [lax.rem(base + 16 + p, nmd) for p in (15, 12)],
        3: [spot[15], ahead],
        12: [spot[0], behind],
    }
    for p in more:
        @pl.when(place == p)
        def _(p=p):
            for m in more[p]:
                pl.semaphore_signal(barrier, inc=1, device_id=(m, th), device_id_type=MESH)

    lane = lax.broadcasted_iota(jnp.int32, (8, LANES), 1)
    sub = lax.broadcasted_iota(jnp.int32, (8, LANES), 0)

    def remote(src, dst, s, r, dev):
        return pltpu.make_async_remote_copy(
            src_ref=src, dst_ref=dst, send_sem=s, recv_sem=r, device_id=dev, device_id_type=MESH)

    def rows8(z):
        return pl.ds(pl.multiple_of(z * 8, 8), 8)

    def pack_columns(step, s):
        east = west = jnp.zeros((8, LANES), jnp.float32)
        for x in range(2):
            for zc in range(16):
                k = x * 16 + zc
                c = Q[step][s, x + 1, 8 + zc * 8:16 + zc * 8, :]
                east = jnp.where(lane == k, pltpu.roll(c, k + 1, 1), east)
                west = jnp.where(lane == k, pltpu.roll(c, k, 1) if k else c, west)
        YP[step, s, 0] = east
        YP[step, s, 1] = west

    def fine_copies(step, s):
        q = Q[step]
        return [
            remote(q.at[s, 2, 8:136, :], q.at[s, 0, 8:136, :], q_s.at[step, s, 0], q_r.at[step, s, 0], (right, th)),
            remote(q.at[s, 1, 8:136, :], q.at[s, 3, 8:136, :], q_s.at[step, s, 1], q_r.at[step, s, 1], (left, th)),
            remote(YP.at[step, s, 0], YW.at[step, s], y_s.at[step, s, 0], y_r.at[step, s, 0], (md, up)),
            remote(YP.at[step, s, 1], YE.at[step, s], y_s.at[step, s, 1], y_r.at[step, s, 1], (md, dn)),
        ]

    def start_rows(step, s):
        for c in fine_copies(step, s)[2:]:
            c.start()

    def start_planes(step, s):
        q = Q[step]
        copies = fine_copies(step, s)
        for side, plane in ((0, 2), (1, 1)):
            a, b, c = [by_way[side][w] for w in (0, 1, 1)]
            via = source[side] & (s < RELAYED)
            dev = jnp.where(s == 0, a, jnp.where(s == 1, b, c))

            @pl.when(via)
            def _():
                remote(q.at[s, plane, 8:136, :], QB.at[step, side], q_s.at[step, s, side], qb_r.at[step, side], (dev, th)).start()

            @pl.when(jnp.logical_not(via))
            def _():
                copies[side].start()

    def fine_forward(step, side):
        k = species_of[side]
        return remote(QB.at[step, side], Q[step].at[k, 3 * side, 8:136, :], qf_s.at[step, side], q_r.at[step, k, side], (target[side], th))

    def forward_fines(step):
        for side in range(2):
            @pl.when(relays_fines[side])
            def _():
                remote(Q[step].at[0, 1, 8:136, :], QB.at[step, side], qf_s.at[step, side], qb_r.at[step, side], (came_from[side], th)).wait_recv()
                fine_forward(step, side).start()

    loads[1].wait()
    for t in range(NT):
        S[:, t] = M[:, :, t * LANES:(t + 1) * LANES].astype(jnp.float32)

    my_rows = pl.ds(pl.multiple_of(th * 32, 32), 32)
    for x in range(2):
        Sall[x, my_rows, :] = S[x, th]

    def put(e, x, t, z, out):
        rows = slice(8 + z * 8, 16 + z * 8)
        r = R[e]
        for i in range(19):
            cy = VELOCITIES[i][1]
            k = SLOT[i]
            if cy == 0:
                r[k, x + 1, t, rows, :] = out[i]
            elif cy == 1:
                v = pltpu.roll(out[i], 1, 1)
                r[k, x + 1, t, rows, 1:LANES] = v[:, 1:LANES]
                r[k, x + 1, lax.rem(t + 1, NT), rows, 0:1] = v[:, 0:1]
            else:
                v = pltpu.roll(out[i], LANES - 1, 1)
                r[k, x + 1, t, rows, 0:LANES - 1] = v[:, 0:LANES - 1]
                r[k, x + 1, lax.rem(t + 3, NT), rows, LANES - 1:LANES] = v[:, LANES - 1:LANES]
        if z == 0:
            B[0, x * NT + t] = out[16]
            B[1, x * NT + t] = out[17]

    def solid_at(x, t, z):
        return S[x, t, z * 8:z * 8 + 8, :] > 0

    def chunks(z, body):
        def step(t, _):
            for x in range(2):
                body(x, t, z)
            return 0
        lax.fori_loop(0, NT, step, 0)

    def tile(t):
        return pl.ds(pl.multiple_of(t * LANES, LANES), LANES)

    def pull(e, x, t, z):
        f = []
        for i in range(19):
            cx, _, cz = VELOCITIES[i]
            f.append(R[e][SLOT[i], x + 1 - cx, t, 8 + z * 8 - cz:16 + z * 8 - cz, :])
        return f

    def quarter(e, side, z):
        r = R[e]
        rows = slice(8 + z * 8, 16 + z * 8)
        slots = slice(5 * side, 5 * side + 5)
        return remote(
            r.at[slots, 2 - side, :, rows, :], r.at[slots, 3 * side, :, rows, :],
            xs_s.at[e, side, z], xs_r.at[e, side, z], ((right, left)[side], th))

    def rim_copies(e):
        return [
            remote(ZU.at[e], RU.at[e, 0:5], zs_s.at[e, 0], zs_r.at[e, 0], (md, up)),
            remote(ZU.at[e, 3], RU.at[e, 5], zs_s.at[e, 1], zs_r.at[e, 1], (right, up)),
            remote(ZU.at[e, 4], RU.at[e, 6], zs_s.at[e, 2], zs_r.at[e, 2], (left, up)),
            remote(ZD.at[e], RD.at[e, 0:5], zs_s.at[e, 3], zs_r.at[e, 3], (md, dn)),
            remote(ZD.at[e, 4], RD.at[e, 5], zs_s.at[e, 4], zs_r.at[e, 4], (right, dn)),
            remote(ZD.at[e, 3], RD.at[e, 6], zs_s.at[e, 5], zs_r.at[e, 5], (left, dn)),
        ]

    def send(e, z):
        r = R[e]
        if z in (3, 0):
            pack, list_, row = (ZU, UP, 39) if z == 3 else (ZD, DOWN, 8)
            for k in range(5):
                for x in range(2):
                    for t in range(NT):
                        n = x * NT + t
                        pack[e, k, n:n + 1, :] = r[SLOT[list_[k]], x + 1, t, row:row + 1, :]
            for c in rim_copies(e)[0 if z == 3 else 3:][:3]:
                c.start()
        rows = slice(8 + z * 8, 16 + z * 8)
        for side in range(2):
            c = quarter(e, side, z)
            if WAYS[z] is None:
                c.start()
                continue

            @pl.when(source[side])
            def _():
                slots = slice(5 * side, 5 * side + 5)
                remote(r.at[slots, 2 - side, :, rows, :], RB.at[e, side], xs_s.at[e, side, z], rb_r.at[e, side], (by_way[side][WAYS[z]], th)).start()

            @pl.when(jnp.logical_not(source[side]))
            def _():
                c.start()

    def forward(e, side):
        z = quarter_of[side]
        rows = pl.ds(pl.multiple_of(8 + z * 8, 8), 8)
        slots = slice(5 * side, 5 * side + 5)
        return remote(RB.at[e, side], R[e].at[slots, 3 * side, :, rows, :], fw_s.at[e, side], xs_r.at[e, side, z], (target[side], th))

    def relay(e):
        for side in range(2):
            @pl.when(relays_flow[side])
            def _():
                slots = slice(5 * side, 5 * side + 5)
                remote(R[e].at[slots, 2 - side, :, 8:16, :], RB.at[e, side], fw_s.at[e, side], rb_r.at[e, side], (came_from[side], th)).wait_recv()
                forward(e, side).start()

    def rims(e, vertical):
        for c in rim_copies(e)[3 * vertical:3 * vertical + 3]:
            c.wait_recv()
        low = sub < NT
        is_open = W[...] == 1
        src = RD if vertical else RU
        for k in range(5):
            pop = DOWN[k] if vertical else UP[k]
            cx = VELOCITIES[pop][0]
            rim = src[e, k]
            if cx == 1:
                rim = pltpu.roll(jnp.where(low, rim, src[e, 5]), NT, 0)
            elif cx == -1:
                rim = pltpu.roll(jnp.where(low, src[e, 6], rim), NT, 0)
            if vertical:
                rim = jnp.where(th == 3, WEIGHTS[pop] * INLET_DENSITY, rim)
                row = 40
            else:
                if VELOCITIES[pop][1] == 0:
                    wall = ZD[e, k]
                else:
                    wall = jnp.concatenate([B[k - 1, n, 0:1, :] for n in range(8)], axis=0)
                wall = jnp.where(is_open, WEIGHTS[pop] * OUTLET_DENSITY, wall)
                rim = jnp.where(th == 0, wall, rim)
                row = 7
            for x in range(2):
                for t in range(NT):
                    n = x * NT + t
                    R[e][SLOT[pop], x + 1 - cx, t, row:row + 1, :] = rim[n:n + 1, :]

    def arrive(e, z):
        if z == 3:
            quarter(e, 0, 3).wait_recv()
            quarter(e, 1, 3).wait_recv()
            rims(e, 1)
        if z > 0:
            quarter(e, 0, z - 1).wait_recv()
            quarter(e, 1, z - 1).wait_recv()
        else:
            rims(e, 0)

    def await_friends():
        @pl.when(source[0] | source[1])
        def _():
            pl.semaphore_wait(barrier, len(friends) + 5)

        @pl.when((place == 3) | (place == 12))
        def _():
            pl.semaphore_wait(barrier, len(friends) + 2)

        @pl.when(jnp.logical_not(is_relay[0] | is_relay[1]))
        def _():
            pl.semaphore_wait(barrier, len(friends))

    def flow_first(x, t, z):
        rows = slice(z * 8, z * 8 + 8)
        put(0, x, t, z, collide([F[i, x, rows, tile(t)] for i in range(19)], solid_at(x, t, z)))

    solids = [
        remote(S.at[:, p], Sall.at[:, my_rows, :], ss_s.at[k], ss_r.at[k], (md, p))
        for k, p in enumerate(peers)
    ]
    def planes(s, _):
        start_planes(0, s)
        return 0

    for z in QUARTERS:
        loads[2 + QUARTERS.index(z)].wait()
        chunks(z, flow_first)
        if z == 3:
            await_friends()
        send(0, z)
    loads[0].wait()
    lax.fori_loop(0, 4, planes, 0)
    relay(0)
    forward_fines(0)

    def pack_first(s, _):
        pack_columns(0, s)
        return 0

    lax.fori_loop(0, 4, pack_first, 0)

    def send_rows(s, _):
        start_rows(0, s)
        return 0

    lax.fori_loop(0, 4, send_rows, 0)
    for c in solids:
        c.start()
    for c in small:
        c.wait()
    for x in range(2):
        for t in range(NT):
            W[x * NT + t:x * NT + t + 1, :] = wire[x:x + 1, t * LANES:(t + 1) * LANES]


    def inverse(s, _):
        d = jnp.full((8, LANES), diff[s], jnp.float32)
        h = 0.5 * lax.rsqrt(d)
        theta = -2.0 * jnp.log1p(h + h * h / (1.0 + jnp.sqrt(1.0 + h * h)))
        j = lane.astype(jnp.float32)
        full = 2.0 * LANES
        norm = 1.0 / (jnp.sqrt(4.0 * d + 1.0) * (1.0 - jnp.exp(theta * full)))
        for zc in range(16):
            i = (sub + zc * 8).astype(jnp.float32)
            gap = jnp.abs(i - j)
            away = i + j + 1.0
            g = jnp.exp(theta * gap) + jnp.exp(theta * (full - gap))
            g = g + (jnp.exp(theta * away) + jnp.exp(theta * (full - away)))
            G[zc * 8:zc * 8 + 8, :] = g * norm
        g = G[...]
        hi = g.astype(jnp.bfloat16)
        GB[s, :, 0:LANES] = hi
        GB[s, :, LANES:2 * LANES] = (g - hi.astype(jnp.float32)).astype(jnp.bfloat16)
        return 0

    lax.fori_loop(0, 4, inverse, 0)

    def flow_second(x, t, z):
        put(1, x, t, z, collide(pull(0, x, t, z), solid_at(x, t, z)))

    for z in QUARTERS:
        arrive(0, z)
        chunks(z, flow_second)
        send(1, z)

    relay(1)

    def flow_last(x, t, z):
        f = pull(1, x, t, z)
        rows = slice(z * 8, z * 8 + 8)
        for i in range(19):
            pops_out[i, x, rows, tile(t)] = f[i]
        _, _, mass, flux = pair_moments(f)
        fluid = (1.0 - S[x, t, rows, :]) / mass
        for a in range(3):
            V[a, x, t, rows, :] = flux[a] * fluid

    def speeds(z):
        there = pl.ds(pl.multiple_of(th * 32 + z * 8, 8), 8)
        return [
            remote(V.at[:, :, p, z * 8:z * 8 + 8, :], Vall.at[:, :, there, :], vs_s.at[k, z], vs_r.at[k, z], (md, p))
            for k, p in enumerate(peers)
        ]

    for z in QUARTERS:
        arrive(1, z)
        chunks(z, flow_last)
        for c in speeds(z):
            c.start()
    for a in range(3):
        for x in range(2):
            Vall[a, x, my_rows, :] = V[a, x, th]

    for c in solids:
        c.wait_send()
    for e in range(2):
        for c in rim_copies(e):
            c.wait_send()
        for z in QUARTERS:
            for side in range(2):
                quarter(e, side, z).wait_send()
    for s in range(4):
        for c in fine_copies(0, s):
            c.wait_send()

    for c in solids:
        c.wait_recv()
    for z in QUARTERS:
        for c in speeds(z):
            c.wait_recv()

    def coefficients(n, _):
        for x in range(2):
            for m in range(4):
                rows = rows8(n * 4 + m)
                ux, uy, uz = [Vall[a, x, rows, :] for a in range(3)]
                C[0, x, rows, :] = (1.0 - 4.0 * LATERAL_DIFFUSION) - (jnp.abs(ux) + jnp.abs(uy) + jnp.abs(uz))
                C[1, x, rows, :] = LATERAL_DIFFUSION + jnp.maximum(ux, 0.0)
                C[2, x, rows, :] = LATERAL_DIFFUSION - jnp.minimum(ux, 0.0)
                C[3, x, rows, :] = LATERAL_DIFFUSION + jnp.maximum(uy, 0.0)
                C[4, x, rows, :] = LATERAL_DIFFUSION - jnp.minimum(uy, 0.0)
                C[5, x, rows, :] = jnp.maximum(uz, 0.0)
                C[6, x, rows, :] = -jnp.minimum(uz, 0.0)
        return 0

    lax.fori_loop(0, 4, coefficients, 0)

    def transport(step, s):
        q = Q[step]
        for x in range(2):
            q[s, x + 1, 7:8, :] = q[s, x + 1, 8:9, :]
            q[s, x + 1, 136:137, :] = q[s, x + 1, 135:136, :]
        for c in fine_copies(step, s):
            c.wait_recv()
        west_in = YW[step, s]
        east_in = YE[step, s]
        kept = ret[s]
        for x in range(2):
            for zc in range(16):
                n = x * 16 + zc
                rows = slice(zc * 8, zc * 8 + 8)
                held = slice(zc * 8 + 8, zc * 8 + 16)
                c = q[s, x + 1, held, :]
                below = q[s, x + 1, zc * 8 + 7:zc * 8 + 15, :]
                above = q[s, x + 1, zc * 8 + 9:zc * 8 + 17, :]
                from_west = pltpu.roll(west_in, LANES - n, 1) if n else west_in
                from_east = pltpu.roll(east_in, LANES - 1 - n, 1)
                south = jnp.where(lane == 0, from_west, pltpu.roll(c, 1, 1))
                north = jnp.where(lane == LANES - 1, from_east, pltpu.roll(c, LANES - 1, 1))
                X[rows, x * LANES:(x + 1) * LANES] = total([
                    c * (C[0, x, rows, :] - kept * Sall[x, rows, :]),
                    q[s, x, held, :] * C[1, x, rows, :],
                    q[s, x + 2, held, :] * C[2, x, rows, :],
                    south * C[3, x, rows, :],
                    north * C[4, x, rows, :],
                    below * C[5, x, rows, :],
                    above * C[6, x, rows, :],
                ])
        v = X[...]
        v_hi = v.astype(jnp.bfloat16)
        v_lo = (v - v_hi.astype(jnp.float32)).astype(jnp.bfloat16)
        out = jnp.dot(GB[s], jnp.concatenate([v_hi, v_hi], axis=0), preferred_element_type=jnp.float32)
        out += jnp.dot(GB[s, :, 0:LANES], v_lo, preferred_element_type=jnp.float32)
        for x in range(2):
            part = out[:, x * LANES:(x + 1) * LANES]
            if step == 0:
                Q1[s, x + 1, 8:136, :] = part
            else:
                fines_out[s, x] = part

    def transport_first(s, _):
        transport(0, s)
        start_planes(1, s)
        pack_columns(1, s)
        start_rows(1, s)
        return 0

    lax.fori_loop(0, 4, transport_first, 0)
    forward_fines(1)

    def transport_second(s, _):
        transport(1, s)
        return 0

    lax.fori_loop(0, 4, transport_second, 0)

    for s in range(4):
        for c in fine_copies(1, s):
            c.wait_send()
    for z in QUARTERS:
        for c in speeds(z):
            c.wait_send()
    for step in range(2):
        for side in range(2):
            @pl.when(relays_flow[side])
            def _():
                forward(step, side).wait_send()

            @pl.when(relays_fines[side])
            def _():
                fine_forward(step, side).wait_send()


def put_out_kernel(a, b, a_out, b_out, sem):
    copies = [
        pltpu.make_async_copy(a.at[:, :, z * 8:z * 8 + 8, :], a_out.at[:, :, z * 8:z * 8 + 8, :], sem.at[z])
        for z in range(4)
    ]
    copies.append(pltpu.make_async_copy(b, b_out, sem.at[4]))
    for c in copies:
        c.start()
    for c in copies:
        c.wait()


def put_out(populations_out, fines_out):
    vmem = pl.BlockSpec(memory_space=pltpu.VMEM)
    any_ = pl.BlockSpec(memory_space=pltpu.HBM)
    return pl.pallas_call(
        put_out_kernel,
        out_shape=(
            jax.ShapeDtypeStruct(populations_out.shape, jnp.float32),
            jax.ShapeDtypeStruct(fines_out.shape, jnp.float32),
        ),
        in_specs=[vmem, vmem],
        out_specs=(any_, any_),
        scratch_shapes=[pltpu.SemaphoreType.DMA((5,))],
        compiler_params=pltpu.CompilerParams(vmem_limit_bytes=1024 * 1024),
        name="put_out",
    )(populations_out, fines_out)


def on_device(populations, fibre_mask, wire_open, fines, diffusivity, retention):
    any_ = pl.BlockSpec(memory_space=pl.ANY)
    vmem = pl.BlockSpec(memory_space=pltpu.VMEM)
    f32 = jnp.float32
    dma = pltpu.SemaphoreType.DMA
    populations_out, fines_out = pl.pallas_call(
        kernel,
        out_shape=(
            jax.ShapeDtypeStruct(populations.shape, f32),
            jax.ShapeDtypeStruct(fines.shape, f32),
        ),
        in_specs=[any_] * 6,
        out_specs=(vmem, vmem),
        scratch_shapes=[
            pltpu.VMEM(wire_open.shape, jnp.int32),
            pltpu.SMEM(diffusivity.shape, f32),
            pltpu.SMEM(retention.shape, f32),
            pltpu.VMEM(populations.shape, f32),
            pltpu.VMEM((19, 4, NT, 48, LANES), f32),
            pltpu.VMEM((19, 4, NT, 48, LANES), f32),
            pltpu.VMEM(fibre_mask.shape, jnp.int32),
            pltpu.VMEM((2, NT, 32, LANES), f32),
            pltpu.VMEM((2, 128, LANES), f32),
            pltpu.VMEM((3, 2, NT, 32, LANES), f32),
            pltpu.VMEM((3, 2, 128, LANES), f32),
            pltpu.VMEM((2, 8, 8, LANES), f32),
            pltpu.VMEM((2, 5, 8, LANES), f32),
            pltpu.VMEM((2, 5, 8, LANES), f32),
            pltpu.VMEM((2, 7, 8, LANES), f32),
            pltpu.VMEM((2, 7, 8, LANES), f32),
            pltpu.VMEM((8, LANES), jnp.int32),
            pltpu.VMEM((4, 4, 144, LANES), f32),
            pltpu.VMEM((4, 4, 144, LANES), f32),
            pltpu.VMEM((7, 2, 128, LANES), f32),
            pltpu.VMEM((128, 2 * LANES), f32),
            pltpu.VMEM((128, LANES), f32),
            pltpu.VMEM((4, 128, 2 * LANES), jnp.bfloat16),
            pltpu.VMEM((2, 4, 2, 8, LANES), f32),
            pltpu.VMEM((2, 4, 8, LANES), f32),
            pltpu.VMEM((2, 4, 8, LANES), f32),
            pltpu.VMEM((2, 2, 5, NT, 8, LANES), f32),
            pltpu.VMEM((2, 2, 128, LANES), f32),
            dma((9,)),
            dma((2, 2, 4)), dma((2, 2, 4)),
            dma((2, 6)), dma((2, 6)),
            dma((3,)), dma((3,)),
            dma((3, 4)), dma((3, 4)),
            dma((2, 4, 2)), dma((2, 4, 2)),
            dma((2, 4, 2)), dma((2, 4, 2)),
            dma((2, 2)), dma((2, 2)),
            dma((2, 2)), dma((2, 2)),
        ],
        compiler_params=pltpu.CompilerParams(
            collective_id=0, has_side_effects=True, vmem_limit_bytes=48 * 1024 * 1024),
        name="drainage",
    )(*[
        pltpu.with_memory_space_constraint(v, pltpu.HBM)
        for v in (populations, fibre_mask, wire_open, fines, diffusivity, retention)
    ])
    return put_out(populations_out, fines_out)


def solution(mesh):
    return jax.shard_map(
        on_device,
        mesh=mesh,
        in_specs=(
            P(None, "md", "th", None), P("md", "th", None), P("md", None),
            P(None, "md", None, "th"), P(), P(),
        ),
        out_specs=(P(None, "md", "th", None), P(None, "md", None, "th")),
        check_vma=False,
    )
```

```python
import functools

import jax
import jax.numpy as jnp
from jax import lax
from jax.experimental import pallas as pl
from jax.experimental.pallas import tpu as pltpu
from jax.sharding import PartitionSpec as P

VELOCITIES = [
    (0, 0, 0), (1, 0, 0), (-1, 0, 0), (0, 1, 0), (0, -1, 0), (0, 0, 1), (0, 0, -1),
    (1, 1, 0), (-1, -1, 0), (1, -1, 0), (-1, 1, 0), (1, 0, 1), (-1, 0, -1), (1, 0, -1),
    (-1, 0, 1), (0, 1, 1), (0, -1, -1), (0, 1, -1), (0, -1, 1),
]
WEIGHTS = [1.0 / 3.0] + [1.0 / 18.0] * 6 + [1.0 / 36.0] * 12
OPPOSITE = [0, 2, 1, 4, 3, 6, 5, 8, 7, 10, 9, 12, 11, 14, 13, 16, 15, 18, 17]
RELAXATION = 1.6
INLET_DENSITY = 1.03
OUTLET_DENSITY = 0.97
LATERAL_DIFFUSION = 0.1

PLUS = [1, 7, 9, 11, 13]
MINUS = [2, 8, 10, 12, 14]
ZERO = [0, 3, 4, 5, 6, 15, 16, 17, 18]
SLOT = {i: k for k, i in enumerate(PLUS + MINUS + ZERO)}
UP = [5, 15, 18, 11, 14]
DOWN = [6, 16, 17, 12, 13]

MESH = pl.DeviceIdType.MESH
LANES = 128
NT = 4
TOP = 8


def total(items):
    items = list(items)
    while len(items) > 1:
        items = [a + b for a, b in zip(items[::2], items[1::2])] + (
            [items[-1]] if len(items) % 2 else []
        )
    return items[0]


PAIRS = list(range(1, 19, 2))


def signed(terms):
    plus = [v for c, v in terms if c > 0]
    minus = [v for c, v in terms if c < 0]
    return total(plus) - total(minus) if minus else total(plus)


def pair_moments(f):
    even = {i: f[i] + f[i + 1] for i in PAIRS}
    odd = {i: f[i] - f[i + 1] for i in PAIRS}
    mass = total([f[0]] + [even[i] for i in PAIRS])
    flux = [
        signed([(VELOCITIES[i][a], odd[i]) for i in PAIRS if VELOCITIES[i][a]]) for a in range(3)
    ]
    return even, odd, mass, flux


def collide(f, solid):
    even, odd, mass, flux = pair_moments(f)
    scale = (4.5 ** 0.5) / mass
    px, py, pz = [v * scale for v in flux]
    base = 1.0 - (1.0 / 3.0) * (px * px + py * py + pz * pz)
    keep = 1.0 - RELAXATION
    k_even = jnp.where(solid, 0.5, 0.5 * keep)
    k_odd = jnp.where(solid, -0.5, 0.5 * keep)
    m_diag = jnp.where(solid, 0.0, (RELAXATION * WEIGHTS[7]) * mass)
    m_axis = m_diag + m_diag
    odd_diag, odd_axis = (2.0 ** 0.5) * m_diag, (2.0 ** 0.5) * m_axis
    out = [None] * 19
    out[0] = jnp.where(solid, 1.0, keep) * f[0] + (WEIGHTS[0] / WEIGHTS[7]) * (m_diag * base)
    for i in PAIRS:
        p = signed([(c, v) for c, v in zip(VELOCITIES[i], (px, py, pz)) if c])
        axis = i < 7
        a = k_even * even[i] + (m_axis if axis else m_diag) * (base + p * p)
        b = k_odd * odd[i] + (odd_axis if axis else odd_diag) * p
        out[i] = a + b
        out[i + 1] = a - b
    return out


QUARTERS = (3, 2, 1, 0)
WAYS = {3: 0, 2: 1, 1: None, 0: None}
RELAYED = 2


def kernel(
    pops, mask, wire_hbm, fines, diff_hbm, ret_hbm, pops_out, fines_out,
    wire, diff, ret, F, R0, R1, M, S, Sall, V, Vall, B, ZU, ZD, RU, RD, W, Q0, Q1, C, X, G, GB, YP, YW, YE, RB, QB,
    in_sem, xs_s, xs_r, zs_s, zs_r, ss_s, ss_r, vs_s, vs_r, q_s, q_r, y_s, y_r,
    rb_r, fw_s, qb_r, qf_s,
):
    md = lax.axis_index("md")
    th = lax.axis_index("th")
    nmd = lax.axis_size("md")
    right, left = lax.rem(md + 1, nmd), lax.rem(md + nmd - 1, nmd)
    up, dn = lax.rem(th + 1, 4), lax.rem(th + 3, 4)
    peers = [lax.rem(th + d, 4) for d in (1, 2, 3)]
    R = (R0, R1)
    Q = (Q0, Q1)
    place = lax.rem(md, 16)
    base = md - place
    spot = {p: lax.rem(base + p, nmd) for p in (0, 3, 12, 15)}
    ahead, behind = lax.rem(base + 16, nmd), lax.rem(base + nmd - 1, nmd)
    by_way = ((spot[0], spot[3]), (spot[15], spot[12]))
    source = (place == 15, place == 0)
    is_relay = ((place == 0) | (place == 3), (place == 15) | (place == 12))
    part = (
        jnp.where(place == 0, 0, jnp.where(place == 3, 1, 2)),
        jnp.where(place == 15, 0, jnp.where(place == 12, 1, 2)),
    )
    quarter_of = [jnp.where(p == 0, 3, jnp.where(p == 1, 2, 0)) for p in part]
    species_of = [jnp.where(p == 0, 0, jnp.where(p == 1, 1, 0)) for p in part]
    relays_flow = [is_relay[side] & ((part[side] == 0) | (part[side] == 1)) for side in range(2)]
    relays_fines = [is_relay[side] & ((part[side] == 0) | (part[side] == 1)) for side in range(2)]
    target = (ahead, behind)
    came_from = (spot[15], spot[0])

    loads = [
        pltpu.make_async_copy(fines, Q0.at[:, 1:3, 8:136, :], in_sem.at[0]),
    ]
    loads.append(pltpu.make_async_copy(mask, M, in_sem.at[1]))
    for z in QUARTERS:
        loads.append(pltpu.make_async_copy(
            pops.at[:, :, z * 8:z * 8 + 8, :], F.at[:, :, z * 8:z * 8 + 8, :], in_sem.at[2 + z]))
    small = [
        pltpu.make_async_copy(a, b, in_sem.at[6 + k])
        for k, (a, b) in enumerate(((wire_hbm, wire), (diff_hbm, diff), (ret_hbm, ret)))
    ]
    for c in loads + small:
        c.start()

    barrier = pltpu.get_barrier_semaphore()
    friends = [(right, th), (left, th)] + [(md, p) for p in peers]
    friends += [(m, t) for m in (right, left) for t in (up, dn)]
    for d in friends:
        pl.semaphore_signal(barrier, inc=1, device_id=d, device_id_type=MESH)

    more = {
        0: [spot[15], spot[12], ahead] + [lax.rem(base + nmd - 16 + p, nmd) for p in (0, 3)],
        15: [spot[0], spot[3], behind] + [lax.rem(base + 16 + p, nmd) for p in (15, 12)],
        3: [spot[15], ahead],
        12: [spot[0], behind],
    }
    for p in more:
        @pl.when(place == p)
        def _(p=p):
            for m in more[p]:
                pl.semaphore_signal(barrier, inc=1, device_id=(m, th), device_id_type=MESH)

    lane = lax.broadcasted_iota(jnp.int32, (8, LANES), 1)
    sub = lax.broadcasted_iota(jnp.int32, (8, LANES), 0)

    def remote(src, dst, s, r, dev):
        return pltpu.make_async_remote_copy(
            src_ref=src, dst_ref=dst, send_sem=s, recv_sem=r, device_id=dev, device_id_type=MESH)

    def rows8(z):
        return pl.ds(pl.multiple_of(z * 8, 8), 8)

    def pack_columns(step, s):
        east = west = jnp.zeros((8, LANES), jnp.float32)
        for x in range(2):
            for zc in range(16):
                k = x * 16 + zc
                c = Q[step][s, x + 1, 8 + zc * 8:16 + zc * 8, :]
                east = jnp.where(lane == k, pltpu.roll(c, k + 1, 1), east)
                west = jnp.where(lane == k, pltpu.roll(c, k, 1) if k else c, west)
        YP[step, s, 0] = east
        YP[step, s, 1] = west

    def fine_copies(step, s):
        q = Q[step]
        return [
            remote(q.at[s, 2, 8:136, :], q.at[s, 0, 8:136, :], q_s.at[step, s, 0], q_r.at[step, s, 0], (right, th)),
            remote(q.at[s, 1, 8:136, :], q.at[s, 3, 8:136, :], q_s.at[step, s, 1], q_r.at[step, s, 1], (left, th)),
            remote(YP.at[step, s, 0], YW.at[step, s], y_s.at[step, s, 0], y_r.at[step, s, 0], (md, up)),
            remote(YP.at[step, s, 1], YE.at[step, s], y_s.at[step, s, 1], y_r.at[step, s, 1], (md, dn)),
        ]

    def start_rows(step, s):
        for c in fine_copies(step, s)[2:]:
            c.start()

    def start_planes(step, s):
        q = Q[step]
        copies = fine_copies(step, s)
        for side, plane in ((0, 2), (1, 1)):
            a, b, c = [by_way[side][w] for w in (0, 1, 1)]
            via = source[side] & (s < RELAYED)
            dev = jnp.where(s == 0, a, jnp.where(s == 1, b, c))

            @pl.when(via)
            def _():
                remote(q.at[s, plane, 8:136, :], QB.at[step, side], q_s.at[step, s, side], qb_r.at[step, side], (dev, th)).start()

            @pl.when(jnp.logical_not(via))
            def _():
                copies[side].start()

    def fine_forward(step, side):
        k = species_of[side]
        return remote(QB.at[step, side], Q[step].at[k, 3 * side, 8:136, :], qf_s.at[step, side], q_r.at[step, k, side], (target[side], th))

    def forward_fines(step):
        for side in range(2):
            @pl.when(relays_fines[side])
            def _():
                remote(Q[step].at[0, 1, 8:136, :], QB.at[step, side], qf_s.at[step, side], qb_r.at[step, side], (came_from[side], th)).wait_recv()
                fine_forward(step, side).start()

    loads[1].wait()
    for t in range(NT):
        S[:, t] = M[:, :, t * LANES:(t + 1) * LANES].astype(jnp.float32)

    my_rows = pl.ds(pl.multiple_of(th * 32, 32), 32)
    for x in range(2):
        Sall[x, my_rows, :] = S[x, th]

    def put(e, x, t, z, out):
        rows = slice(8 + z * 8, 16 + z * 8)
        r = R[e]
        for i in range(19):
            cy = VELOCITIES[i][1]
            k = SLOT[i]
            if cy == 0:
                r[k, x + 1, t, rows, :] = out[i]
            elif cy == 1:
                v = pltpu.roll(out[i], 1, 1)
                r[k, x + 1, t, rows, 1:LANES] = v[:, 1:LANES]
                r[k, x + 1, lax.rem(t + 1, NT), rows, 0:1] = v[:, 0:1]
            else:
                v = pltpu.roll(out[i], LANES - 1, 1)
                r[k, x + 1, t, rows, 0:LANES - 1] = v[:, 0:LANES - 1]
                r[k, x + 1, lax.rem(t + 3, NT), rows, LANES - 1:LANES] = v[:, LANES - 1:LANES]
        if z == 0:
            B[0, x * NT + t] = out[16]
            B[1, x * NT + t] = out[17]

    def solid_at(x, t, z):
        return S[x, t, z * 8:z * 8 + 8, :] > 0

    def chunks(z, body):
        def step(t, _):
            for x in range(2):
                body(x, t, z)
            return 0
        lax.fori_loop(0, NT, step, 0)

    def tile(t):
        return pl.ds(pl.multiple_of(t * LANES, LANES), LANES)

    def pull(e, x, t, z):
        f = []
        for i in range(19):
            cx, _, cz = VELOCITIES[i]
            f.append(R[e][SLOT[i], x + 1 - cx, t, 8 + z * 8 - cz:16 + z * 8 - cz, :])
        return f

    def quarter(e, side, z):
        r = R[e]
        rows = slice(8 + z * 8, 16 + z * 8)
        slots = slice(5 * side, 5 * side + 5)
        return remote(
            r.at[slots, 2 - side, :, rows, :], r.at[slots, 3 * side, :, rows, :],
            xs_s.at[e, side, z], xs_r.at[e, side, z], ((right, left)[side], th))

    def rim_copies(e):
        return [
            remote(ZU.at[e], RU.at[e, 0:5], zs_s.at[e, 0], zs_r.at[e, 0], (md, up)),
            remote(ZU.at[e, 3], RU.at[e, 5], zs_s.at[e, 1], zs_r.at[e, 1], (right, up)),
            remote(ZU.at[e, 4], RU.at[e, 6], zs_s.at[e, 2], zs_r.at[e, 2], (left, up)),
            remote(ZD.at[e], RD.at[e, 0:5], zs_s.at[e, 3], zs_r.at[e, 3], (md, dn)),
            remote(ZD.at[e, 4], RD.at[e, 5], zs_s.at[e, 4], zs_r.at[e, 4], (right, dn)),
            remote(ZD.at[e, 3], RD.at[e, 6], zs_s.at[e, 5], zs_r.at[e, 5], (left, dn)),
        ]

    def send(e, z):
        r = R[e]
        if z in (3, 0):
            pack, list_, row = (ZU, UP, 39) if z == 3 else (ZD, DOWN, 8)
            for k in range(5):
                for x in range(2):
                    for t in range(NT):
                        n = x * NT + t
                        pack[e, k, n:n + 1, :] = r[SLOT[list_[k]], x + 1, t, row:row + 1, :]
            for c in rim_copies(e)[0 if z == 3 else 3:][:3]:
                c.start()
        rows = slice(8 + z * 8, 16 + z * 8)
        for side in range(2):
            c = quarter(e, side, z)
            if WAYS[z] is None:
                c.start()
                continue

            @pl.when(source[side])
            def _():
                slots = slice(5 * side, 5 * side + 5)
                remote(r.at[slots, 2 - side, :, rows, :], RB.at[e, side], xs_s.at[e, side, z], rb_r.at[e, side], (by_way[side][WAYS[z]], th)).start()

            @pl.when(jnp.logical_not(source[side]))
            def _():
                c.start()

    def forward(e, side):
        z = quarter_of[side]
        rows = pl.ds(pl.multiple_of(8 + z * 8, 8), 8)
        slots = slice(5 * side, 5 * side + 5)
        return remote(RB.at[e, side], R[e].at[slots, 3 * side, :, rows, :], fw_s.at[e, side], xs_r.at[e, side, z], (target[side], th))

    def relay(e):
        for side in range(2):
            @pl.when(relays_flow[side])
            def _():
                slots = slice(5 * side, 5 * side + 5)
                remote(R[e].at[slots, 2 - side, :, 8:16, :], RB.at[e, side], fw_s.at[e, side], rb_r.at[e, side], (came_from[side], th)).wait_recv()
                forward(e, side).start()

    def rims(e, vertical):
        for c in rim_copies(e)[3 * vertical:3 * vertical + 3]:
            c.wait_recv()
        low = sub < NT
        is_open = W[...] == 1
        src = RD if vertical else RU
        for k in range(5):
            pop = DOWN[k] if vertical else UP[k]
            cx = VELOCITIES[pop][0]
            rim = src[e, k]
            if cx == 1:
                rim = pltpu.roll(jnp.where(low, rim, src[e, 5]), NT, 0)
            elif cx == -1:
                rim = pltpu.roll(jnp.where(low, src[e, 6], rim), NT, 0)
            if vertical:
                rim = jnp.where(th == 3, WEIGHTS[pop] * INLET_DENSITY, rim)
                row = 40
            else:
                if VELOCITIES[pop][1] == 0:
                    wall = ZD[e, k]
                else:
                    wall = jnp.concatenate([B[k - 1, n, 0:1, :] for n in range(8)], axis=0)
                wall = jnp.where(is_open, WEIGHTS[pop] * OUTLET_DENSITY, wall)
                rim = jnp.where(th == 0, wall, rim)
                row = 7
            for x in range(2):
                for t in range(NT):
                    n = x * NT + t
                    R[e][SLOT[pop], x + 1 - cx, t, row:row + 1, :] = rim[n:n + 1, :]

    def arrive(e, z):
        if z == 3:
            quarter(e, 0, 3).wait_recv()
            quarter(e, 1, 3).wait_recv()
            rims(e, 1)
        if z > 0:
            quarter(e, 0, z - 1).wait_recv()
            quarter(e, 1, z - 1).wait_recv()
        else:
            rims(e, 0)

    def await_friends():
        @pl.when(source[0] | source[1])
        def _():
            pl.semaphore_wait(barrier, len(friends) + 5)

        @pl.when((place == 3) | (place == 12))
        def _():
            pl.semaphore_wait(barrier, len(friends) + 2)

        @pl.when(jnp.logical_not(is_relay[0] | is_relay[1]))
        def _():
            pl.semaphore_wait(barrier, len(friends))

    def flow_first(x, t, z):
        rows = slice(z * 8, z * 8 + 8)
        put(0, x, t, z, collide([F[i, x, rows, tile(t)] for i in range(19)], solid_at(x, t, z)))

    solids = [
        remote(S.at[:, p], Sall.at[:, my_rows, :], ss_s.at[k], ss_r.at[k], (md, p))
        for k, p in enumerate(peers)
    ]
    def planes(s, _):
        start_planes(0, s)
        return 0

    for z in QUARTERS:
        loads[2 + QUARTERS.index(z)].wait()
        chunks(z, flow_first)
        if z == 3:
            await_friends()
        send(0, z)
    loads[0].wait()
    lax.fori_loop(0, 4, planes, 0)
    relay(0)
    forward_fines(0)

    def pack_first(s, _):
        pack_columns(0, s)
        return 0

    lax.fori_loop(0, 4, pack_first, 0)

    def send_rows(s, _):
        start_rows(0, s)
        return 0

    lax.fori_loop(0, 4, send_rows, 0)
    for c in solids:
        c.start()
    for c in small:
        c.wait()
    for x in range(2):
        for t in range(NT):
            W[x * NT + t:x * NT + t + 1, :] = wire[x:x + 1, t * LANES:(t + 1) * LANES]


    def inverse(s, _):
        d = jnp.full((8, LANES), diff[s], jnp.float32)
        h = 0.5 * lax.rsqrt(d)
        theta = -2.0 * jnp.log1p(h + h * h / (1.0 + jnp.sqrt(1.0 + h * h)))
        j = lane.astype(jnp.float32)
        full = 2.0 * LANES
        norm = 1.0 / (jnp.sqrt(4.0 * d + 1.0) * (1.0 - jnp.exp(theta * full)))
        for zc in range(16):
            i = (sub + zc * 8).astype(jnp.float32)
            gap = jnp.abs(i - j)
            away = i + j + 1.0
            g = jnp.exp(theta * gap) + jnp.exp(theta * (full - gap))
            g = g + (jnp.exp(theta * away) + jnp.exp(theta * (full - away)))
            G[zc * 8:zc * 8 + 8, :] = g * norm
        g = G[...]
        hi = g.astype(jnp.bfloat16)
        GB[s, :, 0:LANES] = hi
        GB[s, :, LANES:2 * LANES] = (g - hi.astype(jnp.float32)).astype(jnp.bfloat16)
        return 0

    lax.fori_loop(0, 4, inverse, 0)

    def flow_second(x, t, z):
        put(1, x, t, z, collide(pull(0, x, t, z), solid_at(x, t, z)))

    for z in QUARTERS:
        arrive(0, z)
        chunks(z, flow_second)
        send(1, z)

    relay(1)

    def flow_last(x, t, z):
        f = pull(1, x, t, z)
        rows = slice(z * 8, z * 8 + 8)
        for i in range(19):
            pops_out[i, x, rows, tile(t)] = f[i]
        _, _, mass, flux = pair_moments(f)
        fluid = (1.0 - S[x, t, rows, :]) / mass
        for a in range(3):
            V[a, x, t, rows, :] = flux[a] * fluid

    def speeds(z):
        there = pl.ds(pl.multiple_of(th * 32 + z * 8, 8), 8)
        return [
            remote(V.at[:, :, p, z * 8:z * 8 + 8, :], Vall.at[:, :, there, :], vs_s.at[k, z], vs_r.at[k, z], (md, p))
            for k, p in enumerate(peers)
        ]

    for z in QUARTERS:
        arrive(1, z)
        chunks(z, flow_last)
        for c in speeds(z):
            c.start()
    for a in range(3):
        for x in range(2):
            Vall[a, x, my_rows, :] = V[a, x, th]

    for c in solids:
        c.wait_send()
    for e in range(2):
        for c in rim_copies(e):
            c.wait_send()
        for z in QUARTERS:
            for side in range(2):
                quarter(e, side, z).wait_send()
    for s in range(4):
        for c in fine_copies(0, s):
            c.wait_send()

    for c in solids:
        c.wait_recv()
    for z in QUARTERS:
        for c in speeds(z):
            c.wait_recv()

    def coefficients(n, _):
        for x in range(2):
            for m in range(4):
                rows = rows8(n * 4 + m)
                ux, uy, uz = [Vall[a, x, rows, :] for a in range(3)]
                C[0, x, rows, :] = (1.0 - 4.0 * LATERAL_DIFFUSION) - (jnp.abs(ux) + jnp.abs(uy) + jnp.abs(uz))
                C[1, x, rows, :] = LATERAL_DIFFUSION + jnp.maximum(ux, 0.0)
                C[2, x, rows, :] = LATERAL_DIFFUSION - jnp.minimum(ux, 0.0)
                C[3, x, rows, :] = LATERAL_DIFFUSION + jnp.maximum(uy, 0.0)
                C[4, x, rows, :] = LATERAL_DIFFUSION - jnp.minimum(uy, 0.0)
                C[5, x, rows, :] = jnp.maximum(uz, 0.0)
                C[6, x, rows, :] = -jnp.minimum(uz, 0.0)
        return 0

    lax.fori_loop(0, 4, coefficients, 0)

    def transport(step, s):
        q = Q[step]
        for x in range(2):
            q[s, x + 1, 7:8, :] = q[s, x + 1, 8:9, :]
            q[s, x + 1, 136:137, :] = q[s, x + 1, 135:136, :]
        for c in fine_copies(step, s):
            c.wait_recv()
        west_in = YW[step, s]
        east_in = YE[step, s]
        kept = ret[s]
        for x in range(2):
            for zc in range(16):
                n = x * 16 + zc
                rows = slice(zc * 8, zc * 8 + 8)
                held = slice(zc * 8 + 8, zc * 8 + 16)
                c = q[s, x + 1, held, :]
                below = q[s, x + 1, zc * 8 + 7:zc * 8 + 15, :]
                above = q[s, x + 1, zc * 8 + 9:zc * 8 + 17, :]
                from_west = pltpu.roll(west_in, LANES - n, 1) if n else west_in
                from_east = pltpu.roll(east_in, LANES - 1 - n, 1)
                south = jnp.where(lane == 0, from_west, pltpu.roll(c, 1, 1))
                north = jnp.where(lane == LANES - 1, from_east, pltpu.roll(c, LANES - 1, 1))
                X[0, rows, x * LANES:(x + 1) * LANES] = total([
                    c * (C[0, x, rows, :] - kept * Sall[x, rows, :]),
                    q[s, x, held, :] * C[1, x, rows, :],
                    q[s, x + 2, held, :] * C[2, x, rows, :],
                    south * C[3, x, rows, :],
                    north * C[4, x, rows, :],
                    below * C[5, x, rows, :],
                    above * C[6, x, rows, :],
                ])
        v = X[0]
        v_hi = v.astype(jnp.bfloat16)
        v_lo = (v - v_hi.astype(jnp.float32)).astype(jnp.bfloat16)
        out = jnp.dot(GB[s], jnp.concatenate([v_hi, v_hi], axis=0), preferred_element_type=jnp.float32)
        out += jnp.dot(GB[s, :, 0:LANES], v_lo, preferred_element_type=jnp.float32)
        for x in range(2):
            part = out[:, x * LANES:(x + 1) * LANES]
            if step == 0:
                Q1[s, x + 1, 8:136, :] = part
            else:
                fines_out[s, x] = part

    def transport_pair(step, s):
        q = Q[step]
        for m in range(2):
            for x in range(2):
                q[s + m, x + 1, 7:8, :] = q[s + m, x + 1, 8:9, :]
                q[s + m, x + 1, 136:137, :] = q[s + m, x + 1, 135:136, :]
            for c in fine_copies(step, s + m):
                c.wait_recv()
        for m in range(2):
            explicit(step, q, s + m, X.at[m])
        for m in range(2):
            out = implicit(s + m, X.at[m])
            for x in range(2):
                lanes = out[:, x * LANES:(x + 1) * LANES]
                if step == 0:
                    Q1[s + m, x + 1, 8:136, :] = lanes
                else:
                    fines_out[s + m, x] = lanes

    def explicit(step, q, s, into):
        west_in = YW[step, s]
        east_in = YE[step, s]
        kept = ret[s]
        for x in range(2):
            for zc in range(16):
                n = x * 16 + zc
                rows = slice(zc * 8, zc * 8 + 8)
                held = slice(zc * 8 + 8, zc * 8 + 16)
                c = q[s, x + 1, held, :]
                below = q[s, x + 1, zc * 8 + 7:zc * 8 + 15, :]
                above = q[s, x + 1, zc * 8 + 9:zc * 8 + 17, :]
                from_west = pltpu.roll(west_in, LANES - n, 1) if n else west_in
                from_east = pltpu.roll(east_in, LANES - 1 - n, 1)
                south = jnp.where(lane == 0, from_west, pltpu.roll(c, 1, 1))
                north = jnp.where(lane == LANES - 1, from_east, pltpu.roll(c, LANES - 1, 1))
                into[rows, x * LANES:(x + 1) * LANES] = total([
                    c * (C[0, x, rows, :] - kept * Sall[x, rows, :]),
                    q[s, x, held, :] * C[1, x, rows, :],
                    q[s, x + 2, held, :] * C[2, x, rows, :],
                    south * C[3, x, rows, :],
                    north * C[4, x, rows, :],
                    below * C[5, x, rows, :],
                    above * C[6, x, rows, :],
                ])

    def implicit(s, values):
        v = values[...]
        v_hi = v.astype(jnp.bfloat16)
        v_lo = (v - v_hi.astype(jnp.float32)).astype(jnp.bfloat16)
        out = jnp.dot(GB[s], jnp.concatenate([v_hi, v_hi], axis=0), preferred_element_type=jnp.float32)
        return out + jnp.dot(GB[s, :, 0:LANES], v_lo, preferred_element_type=jnp.float32)

    def transport_first(s, _):
        transport(0, s)
        start_planes(1, s)
        pack_columns(1, s)
        start_rows(1, s)
        return 0

    lax.fori_loop(0, 4, transport_first, 0)
    forward_fines(1)

    def transport_second(n, _):
        transport_pair(1, 2 * n)
        return 0

    lax.fori_loop(0, 2, transport_second, 0)

    for s in range(4):
        for c in fine_copies(1, s):
            c.wait_send()
    for z in QUARTERS:
        for c in speeds(z):
            c.wait_send()
    for step in range(2):
        for side in range(2):
            @pl.when(relays_flow[side])
            def _():
                forward(step, side).wait_send()

            @pl.when(relays_fines[side])
            def _():
                fine_forward(step, side).wait_send()


def put_out_kernel(a, b, a_out, b_out, sem):
    copies = [
        pltpu.make_async_copy(a.at[:, :, z * 8:z * 8 + 8, :], a_out.at[:, :, z * 8:z * 8 + 8, :], sem.at[z])
        for z in range(4)
    ]
    copies.append(pltpu.make_async_copy(b, b_out, sem.at[4]))
    for c in copies:
        c.start()
    for c in copies:
        c.wait()


def put_out(populations_out, fines_out):
    vmem = pl.BlockSpec(memory_space=pltpu.VMEM)
    any_ = pl.BlockSpec(memory_space=pltpu.HBM)
    return pl.pallas_call(
        put_out_kernel,
        out_shape=(
            jax.ShapeDtypeStruct(populations_out.shape, jnp.float32),
            jax.ShapeDtypeStruct(fines_out.shape, jnp.float32),
        ),
        in_specs=[vmem, vmem],
        out_specs=(any_, any_),
        scratch_shapes=[pltpu.SemaphoreType.DMA((5,))],
        compiler_params=pltpu.CompilerParams(vmem_limit_bytes=1024 * 1024),
        name="put_out",
    )(populations_out, fines_out)


def on_device(populations, fibre_mask, wire_open, fines, diffusivity, retention):
    any_ = pl.BlockSpec(memory_space=pl.ANY)
    vmem = pl.BlockSpec(memory_space=pltpu.VMEM)
    f32 = jnp.float32
    dma = pltpu.SemaphoreType.DMA
    populations_out, fines_out = pl.pallas_call(
        kernel,
        out_shape=(
            jax.ShapeDtypeStruct(populations.shape, f32),
            jax.ShapeDtypeStruct(fines.shape, f32),
        ),
        in_specs=[any_] * 6,
        out_specs=(vmem, vmem),
        scratch_shapes=[
            pltpu.VMEM(wire_open.shape, jnp.int32),
            pltpu.SMEM(diffusivity.shape, f32),
            pltpu.SMEM(retention.shape, f32),
            pltpu.VMEM(populations.shape, f32),
            pltpu.VMEM((19, 4, NT, 48, LANES), f32),
            pltpu.VMEM((19, 4, NT, 48, LANES), f32),
            pltpu.VMEM(fibre_mask.shape, jnp.int32),
            pltpu.VMEM((2, NT, 32, LANES), f32),
            pltpu.VMEM((2, 128, LANES), f32),
            pltpu.VMEM((3, 2, NT, 32, LANES), f32),
            pltpu.VMEM((3, 2, 128, LANES), f32),
            pltpu.VMEM((2, 8, 8, LANES), f32),
            pltpu.VMEM((2, 5, 8, LANES), f32),
            pltpu.VMEM((2, 5, 8, LANES), f32),
            pltpu.VMEM((2, 7, 8, LANES), f32),
            pltpu.VMEM((2, 7, 8, LANES), f32),
            pltpu.VMEM((8, LANES), jnp.int32),
            pltpu.VMEM((4, 4, 144, LANES), f32),
            pltpu.VMEM((4, 4, 144, LANES), f32),
            pltpu.VMEM((7, 2, 128, LANES), f32),
            pltpu.VMEM((2, 128, 2 * LANES), f32),
            pltpu.VMEM((128, LANES), f32),
            pltpu.VMEM((4, 128, 2 * LANES), jnp.bfloat16),
            pltpu.VMEM((2, 4, 2, 8, LANES), f32),
            pltpu.VMEM((2, 4, 8, LANES), f32),
            pltpu.VMEM((2, 4, 8, LANES), f32),
            pltpu.VMEM((2, 2, 5, NT, 8, LANES), f32),
            pltpu.VMEM((2, 2, 128, LANES), f32),
            dma((9,)),
            dma((2, 2, 4)), dma((2, 2, 4)),
            dma((2, 6)), dma((2, 6)),
            dma((3,)), dma((3,)),
            dma((3, 4)), dma((3, 4)),
            dma((2, 4, 2)), dma((2, 4, 2)),
            dma((2, 4, 2)), dma((2, 4, 2)),
            dma((2, 2)), dma((2, 2)),
            dma((2, 2)), dma((2, 2)),
        ],
        compiler_params=pltpu.CompilerParams(
            collective_id=0, has_side_effects=True, vmem_limit_bytes=48 * 1024 * 1024),
        name="drainage",
    )(*[
        pltpu.with_memory_space_constraint(v, pltpu.HBM)
        for v in (populations, fibre_mask, wire_open, fines, diffusivity, retention)
    ])
    return put_out(populations_out, fines_out)


def solution(mesh):
    return jax.shard_map(
        on_device,
        mesh=mesh,
        in_specs=(
            P(None, "md", "th", None), P("md", "th", None), P("md", None),
            P(None, "md", None, "th"), P(), P(),
        ),
        out_specs=(P(None, "md", "th", None), P(None, "md", None, "th")),
        check_vma=False,
    )
```
